32 devices in a mesh: rows: 16 (over z, y, core), cols: 2 (over x).
Axes of the slice: x: 2, y: 2, z: 4, core: 2. Of those that a mesh axis runs over, the one named last changes fastest.
Arguments:
- sketch: bfloat16 [262144, 1024], P('rows', 'cols'), may hold values from -150 to 150
- stiffness: float32 [262144], P('rows'), may hold values from 0.05 to 0.4
- reaction: float32 [262144], P('rows'), may hold values from 0.3 to 3
- panel_order: int32 [8], replicated, may hold values from 0 to 7, each once
Outputs:
- residual: bfloat16 [262144, 1024], P('rows', 'cols')
- basis_rows: bfloat16 [262144, 256], P(('rows', 'cols'))
- factor_cols: float32 [1024, 256], P('cols')
The draws below stay inside these ranges and needn't reach their ends.
All inputs are finite; a program needn't handle non-finite values.
Results may differ from the reference program's by a relative error of at most 0.0071.
Values may be sent and summed in bfloat16 or wider, within the bound.
No kernel may reach another device: no remote copies, remote signals or barrier semaphores. Data moves between devices by JAX's collectives and lax.ppermute only.
A program may use at most 128 MiB of HBM per device.

```python
import math
import jax
import jax.numpy as jnp
from jax import lax

K = 1024
PB = 128
NY = 2048
NPAR = 262144
PANELS = 8


def draw_sketch(key, part):
    noise_key, row_key, col_key = jax.random.split(jax.random.fold_in(key, 11), 3)
    row_pos = jnp.arange(NPAR, dtype=jnp.float32)
    rising = 1.0 + 2.0 * row_pos / NPAR
    row_scale = 0.1 * jnp.exp(math.log(10.0) * jax.random.uniform(row_key, (NPAR,), jnp.float32)) * rising
    col_scale = jnp.exp(math.log(10.0) * jax.random.uniform(col_key, (K,), jnp.float32, -0.5, 0.5))
    noise_field = jnp.clip(jax.random.normal(noise_key, (NPAR, K), jnp.float32), -5.0, 5.0)
    shift_one = PB + PB // 8 + 1
    shift_two = 2 * PB + PB // 4 + 3
    blended = noise_field + 0.5 * jnp.roll(noise_field, shift_one, axis=1) + 0.5 * jnp.roll(noise_field, -shift_two, axis=1)
    return (blended * row_scale[:, None] * col_scale[None, :]).astype(jnp.bfloat16)


def steps_of(rng, extent, cuts, low, high):
    loudness, own = 1.0, jax.random.fold_in(rng, 6)
    for dim, blocks in cuts:
        draws = jnp.exp(jax.random.uniform(jax.random.fold_in(own, dim), (blocks,), jnp.float32, low / len(cuts), high / len(cuts)))
        loudness = loudness * jnp.repeat(draws, extent[dim] // blocks).reshape([-1 if axis == dim else 1 for axis in range(len(extent))])
    return loudness


def setup_inputs(seed: int = 0) -> dict:
    key_list = jax.random.split(jax.random.key(seed), 5)
    return {
        "sketch": draw_sketch(jax.random.fold_in(key_list[4], 71), 0),
        "stiffness": jnp.clip(jnp.exp(math.log(0.4) - 2.0794415 * jax.random.uniform(key_list[1], (NPAR,), jnp.float32) ** steps_of(key_list[1], (NPAR,), ((0, 16),), -0.2, 0.2)), 0.05, 0.4),
        "reaction": jnp.clip(jnp.exp(math.log(3.0) - 2.3025851 * jax.random.uniform(key_list[2], (NPAR,), jnp.float32) ** steps_of(key_list[2], (NPAR,), ((0, 16),), -0.2, 0.2)), 0.3, 3.0),
        "panel_order": jax.random.permutation(key_list[3], PANELS).astype(jnp.int32),
    }


def stencil(cols, stiffness, reaction):
    count = cols.shape[0]
    centre = cols.astype(jnp.float32)
    padded = jnp.pad(centre, ((NY, NY), (0, 0)))
    along_y = jnp.arange(count) % NY
    upward = padded[:count]
    downward = padded[2 * NY:2 * NY + count]
    leftward = jnp.where((along_y == 0)[:, None], 0.0, padded[NY - 1:NY - 1 + count])
    rightward = jnp.where((along_y == NY - 1)[:, None], 0.0, padded[NY + 1:NY + 1 + count])
    mixing = 4.0 * centre - upward - downward - leftward - rightward
    return (reaction[:, None] * centre + stiffness[:, None] * mixing).astype(jnp.bfloat16)

def factorize(gram_full, first_panel, second_panel, cell_total):
    width_all = gram_full.shape[0]
    positions = jnp.arange(width_all, dtype=jnp.int32)[:, None]
    offsets = jnp.arange(PB, dtype=jnp.int32)[None, :]
    ident_one = (positions == first_panel * PB + offsets).astype(jnp.float32)
    ident_two = (positions == second_panel * PB + offsets).astype(jnp.float32)
    core_block = gram_full / cell_total + jnp.concatenate([ident_one, ident_two], 1)
    diag_one = lax.dynamic_slice_in_dim(core_block[:, :PB], (first_panel * PB).astype(jnp.int32), PB, 0)
    lower_one = jnp.linalg.cholesky(diag_one)
    identity = jnp.eye(PB, dtype=lower_one.dtype)
    inverse_one = jax.scipy.linalg.solve_triangular(lower_one, identity, lower=True)
    column_one = jnp.dot(core_block[:, :PB], inverse_one.T, precision=lax.Precision.HIGHEST)
    cross_rows = lax.dynamic_slice_in_dim(column_one, (second_panel * PB).astype(jnp.int32), PB, 0)
    updated = core_block[:, PB:] - jnp.dot(column_one, cross_rows.T, precision=lax.Precision.HIGHEST)
    diag_two = lax.dynamic_slice_in_dim(updated, (second_panel * PB).astype(jnp.int32), PB, 0)
    lower_two = jnp.linalg.cholesky(diag_two)
    inverse_two = jax.scipy.linalg.solve_triangular(lower_two, identity, lower=True)
    column_two = jnp.dot(updated, inverse_two.T, precision=lax.Precision.HIGHEST)
    factor = jnp.concatenate([column_one, column_two], 1)
    return (factor, inverse_one, inverse_two, cross_rows)

def reference(sketch, stiffness, reaction, panel_order):
    first_panel = panel_order[0]
    second_panel = panel_order[1]

    def take(panel_index):
        start = (panel_index * PB).astype(jnp.int32)
        return stencil(lax.dynamic_slice_in_dim(sketch, start, PB, 1), stiffness, reaction)
    panel_one = take(first_panel)
    panel_two = take(second_panel)
    panels_both = jnp.concatenate([panel_one, panel_two], 1)

    def gram_piece(panel_index):
        return jnp.dot(take(panel_index).T.astype(jnp.float32), panels_both.astype(jnp.float32), preferred_element_type=jnp.float32)
    pieces = lax.map(gram_piece, jnp.arange(PANELS, dtype=jnp.int32))
    gram_full = pieces.reshape(K, 2 * PB)
    factor, inverse_one, inverse_two, cross_rows = factorize(gram_full, first_panel, second_panel, NPAR)
    basis_one = jnp.dot(panel_one.astype(jnp.float32), inverse_one.T.astype(jnp.bfloat16).astype(jnp.float32), preferred_element_type=jnp.float32).astype(jnp.bfloat16)
    partial_two = (panel_two.astype(jnp.float32) - jnp.dot(basis_one.astype(jnp.float32), cross_rows.T.astype(jnp.bfloat16).astype(jnp.float32), preferred_element_type=jnp.float32)).astype(jnp.bfloat16)
    basis_two = jnp.dot(partial_two.astype(jnp.float32), inverse_two.T.astype(jnp.bfloat16).astype(jnp.float32), preferred_element_type=jnp.float32).astype(jnp.bfloat16)
    basis_rows = jnp.concatenate([basis_one, basis_two], 1)

    def residual_piece(panel_index):
        weights = lax.dynamic_slice_in_dim(factor, (panel_index * PB).astype(jnp.int32), PB, 0).astype(jnp.bfloat16)
        return (take(panel_index).astype(jnp.float32) - jnp.dot(basis_rows.astype(jnp.float32), weights.T.astype(jnp.float32), preferred_element_type=jnp.float32)).astype(jnp.bfloat16)
    blocks = lax.map(residual_piece, jnp.arange(PANELS, dtype=jnp.int32))
    residual = blocks.transpose(1, 0, 2).reshape(NPAR, K)
    return (residual, basis_rows, factor)
```

```python
import jax
import jax.numpy as jnp
from jax import lax
from jax.experimental import pallas as pl
from jax.experimental.pallas import tpu as pltpu
from jax.sharding import PartitionSpec as P

PB = 128
NY = 2048
LANES = 128
BF16 = jnp.bfloat16
F32 = jnp.float32
HIGHEST = lax.Precision.HIGHEST
SWAP = [(0, 1), (1, 0)]
CELLS_FIRST = (((0,), (0,)), ((), ()))
LAST_LAST = (((1,), (1,)), ((), ()))


def with_halo(block, sides, width):
    for axis, dim in sides:
        count = lax.axis_size(axis)
        forward = [(i, i + 1) for i in range(count - 1)]
        backward = [(target, source) for source, target in forward]
        low = lax.ppermute(
            lax.slice_in_dim(block, block.shape[dim] - width, None, axis=dim), axis, forward
        )
        high = lax.ppermute(lax.slice_in_dim(block, 0, width, axis=dim), axis, backward)
        block = jnp.concatenate([low, block, high], axis=dim)
    return block


def spread(value, axis, source):
    kept = jnp.where(lax.axis_index(axis) == source, value, 0).astype(value.dtype)
    return lax.psum(kept, axis)


def apply_operator(padded, cell_count, sketch, stiffness, reaction):
    centre = sketch.astype(jnp.float32)
    along_y = jnp.arange(cell_count) % NY
    upward = padded[:cell_count].astype(jnp.float32)
    downward = padded[2 * NY : 2 * NY + cell_count].astype(jnp.float32)
    leftward = jnp.where(
        (along_y == 0)[:, None], 0.0, padded[NY - 1 : NY - 1 + cell_count].astype(jnp.float32)
    )
    rightward = jnp.where(
        (along_y == NY - 1)[:, None], 0.0, padded[NY + 1 : NY + 1 + cell_count].astype(jnp.float32)
    )
    mixing = 4.0 * centre - upward - downward - leftward - rightward
    return (reaction[:, None] * centre + stiffness[:, None] * mixing).astype(jnp.bfloat16)


def factorize(gram_full, first_panel, second_panel, cell_total):
    width_all = gram_full.shape[0]
    positions = jnp.arange(width_all, dtype=jnp.int32)[:, None]
    offsets = jnp.arange(PB, dtype=jnp.int32)[None, :]
    ident_one = (positions == first_panel * PB + offsets).astype(jnp.float32)
    ident_two = (positions == second_panel * PB + offsets).astype(jnp.float32)
    core_block = gram_full / cell_total + jnp.concatenate([ident_one, ident_two], 1)
    diag_one = lax.dynamic_slice_in_dim(core_block[:, :PB], first_panel * PB, PB, 0)
    lower_one = jnp.linalg.cholesky(diag_one)
    identity = jnp.eye(PB, dtype=lower_one.dtype)
    inverse_one = jax.scipy.linalg.solve_triangular(lower_one, identity, lower=True)
    column_one = jnp.dot(core_block[:, :PB], inverse_one.T, precision=HIGHEST)
    cross_rows = lax.dynamic_slice_in_dim(column_one, second_panel * PB, PB, 0)
    updated = core_block[:, PB:] - jnp.dot(column_one, cross_rows.T, precision=HIGHEST)
    diag_two = lax.dynamic_slice_in_dim(updated, second_panel * PB, PB, 0)
    lower_two = jnp.linalg.cholesky(diag_two)
    inverse_two = jax.scipy.linalg.solve_triangular(lower_two, identity, lower=True)
    column_two = jnp.dot(updated, inverse_two.T, precision=HIGHEST)
    factor = jnp.concatenate([column_one, column_two], 1)
    return (factor, inverse_one, inverse_two, cross_rows)


def solve_basis(panel_one, panel_two, inverse_one, inverse_two, cross_rows):
    basis_one = jnp.dot(
        panel_one, inverse_one.T.astype(BF16), preferred_element_type=F32
    ).astype(BF16)
    partial_two = (
        panel_two.astype(F32)
        - jnp.dot(basis_one, cross_rows.T.astype(BF16), preferred_element_type=F32)
    ).astype(BF16)
    basis_two = jnp.dot(
        partial_two, inverse_two.T.astype(BF16), preferred_element_type=F32
    ).astype(BF16)
    return jnp.concatenate([basis_one, basis_two], 1)


def any_groups(sketch, stiffness, reaction, panel_order):
    cell_count, local_width = sketch.shape
    padded = with_halo(sketch, (("rows", 0),), NY)
    zfield = apply_operator(padded, cell_count, sketch, stiffness, reaction)
    groups = lax.axis_size("cols")
    own_group = lax.axis_index("cols")
    cell_total = cell_count * lax.axis_size("rows")
    first_panel = panel_order[0]
    second_panel = panel_order[1]
    slice_rows = cell_count // groups
    panels_here = local_width // PB

    def own_panel(panel_index):
        return lax.dynamic_slice_in_dim(zfield, panel_index % panels_here * PB, PB, 1)

    panel_one = spread(own_panel(first_panel), "cols", first_panel // panels_here)
    panel_two = spread(own_panel(second_panel), "cols", second_panel // panels_here)
    panels_both = jnp.concatenate([panel_one, panel_two], 1)
    partial_value = lax.dot_general(zfield, panels_both, CELLS_FIRST, preferred_element_type=F32)
    summed = lax.psum(partial_value, "rows")
    gram_full = lax.all_gather(summed, "cols", axis=0, tiled=True)
    factor, inverse_one, inverse_two, cross_rows = factorize(
        gram_full, first_panel, second_panel, cell_total
    )
    basis_full = solve_basis(panel_one, panel_two, inverse_one, inverse_two, cross_rows)
    own_factor = lax.dynamic_slice_in_dim(factor, own_group * local_width, local_width, 0).astype(
        BF16
    )
    residual = (
        zfield.astype(F32) - jnp.dot(basis_full, own_factor.T, preferred_element_type=F32)
    ).astype(BF16)
    basis_rows = lax.dynamic_slice_in_dim(basis_full, own_group * slice_rows, slice_rows, 0)
    factor_cols = lax.dynamic_slice_in_dim(factor, own_group * local_width, local_width, 0)
    return (residual, basis_rows, factor_cols)


def column_of(row):
    return jnp.transpose(jnp.broadcast_to(row, (LANES, LANES)))


def stencil_piece(piece, pieces, centre_of, up, down, mix_col, stiff_col):
    base = piece * LANES
    lead = 0 if piece == 0 else 16
    tail = 0 if piece == pieces - 1 else 16
    wide = centre_of(base - lead, LANES + lead + tail).astype(F32)
    centre = wide[lead : lead + LANES]
    edge = jnp.zeros((1, LANES), F32)
    if lead:
        left = wide[lead - 1 : lead - 1 + LANES]
    else:
        left = jnp.concatenate([edge, wide[: LANES - 1]], 0)
    if tail:
        right = wide[lead + 1 : lead + 1 + LANES]
    else:
        right = jnp.concatenate([wide[lead + 1 : lead + LANES], edge], 0)
    around = (up.astype(F32) + down.astype(F32)) + (left + right)
    return (mix_col * centre - stiff_col * around).astype(BF16)


def panel_lines(sketch, mix, stiff, lines, tiles, low=None, high=None):
    jobs = lines.shape[0]
    last_line = sketch.shape[0] // NY - 1
    pieces = NY // LANES

    def body(line_ref, tile_ref, up_ref, mid_ref, down_ref, mix_ref, stiff_ref, *rest):
        out_ref = rest[-1]

        def run(above, below):
            for piece in range(pieces):
                at = slice(piece * LANES, (piece + 1) * LANES)
                out_ref[at, :] = stencil_piece(
                    piece,
                    pieces,
                    lambda start, size: mid_ref[start : start + size, :],
                    above[at, :],
                    below[at, :],
                    column_of(mix_ref[piece : piece + 1, :]),
                    column_of(stiff_ref[piece : piece + 1, :]),
                )

        if low is None:
            run(up_ref, down_ref)
        else:
            line = line_ref[pl.program_id(0)]

            @pl.when(line == 0)
            def _():
                run(rest[0], down_ref)

            @pl.when(line == last_line)
            def _():
                run(up_ref, rest[1])

    def block(shift):
        return pl.BlockSpec(
            (NY, LANES), lambda j, ln, tl: (jnp.clip(ln[j] + shift, 0, last_line), tl[j])
        )

    coef = pl.BlockSpec((pieces, LANES), lambda j, ln, tl: (ln[j], 0))
    halo = pl.BlockSpec((NY, LANES), lambda j, ln, tl: (0, tl[j]))
    extra = [] if low is None else [low, high]
    return pl.pallas_call(
        body,
        grid_spec=pltpu.PrefetchScalarGridSpec(
            num_scalar_prefetch=2,
            grid=(jobs,),
            in_specs=[block(-1), block(0), block(1), coef, coef] + [halo] * len(extra),
            out_specs=pl.BlockSpec((NY, LANES), lambda j, ln, tl: (0, j)),
        ),
        out_shape=jax.ShapeDtypeStruct((NY, jobs * LANES), BF16),
        compiler_params=pltpu.CompilerParams(vmem_limit_bytes=24 << 20),
        cost_estimate=pl.CostEstimate(
            flops=jobs * NY * LANES * 8, bytes_accessed=jobs * NY * LANES * 8, transcendentals=0
        ),
        name="panel_lines",
    )(lines, tiles, sketch, sketch, sketch, mix, stiff, *extra)


def full_field(sketch, mix, stiff, low, high):
    cells, width = sketch.shape
    lines = cells // NY
    pieces = NY // LANES

    def body(mid_ref, mix_ref, stiff_ref, low_ref, high_ref, out_ref, mix_wide, stiff_wide):
        @pl.when(pl.program_id(0) == 0)
        def _():
            @pl.loop(0, cells // LANES)
            def _(row):
                at = pl.ds(pl.multiple_of(row * LANES, LANES), LANES)
                mix_wide[at, :] = column_of(mix_ref[pl.ds(row, 1), :])
                stiff_wide[at, :] = column_of(stiff_ref[pl.ds(row, 1), :])

        def run(start, above_of, below_of):
            for piece in range(pieces):
                at = pl.ds(pl.multiple_of(start + piece * LANES, LANES), LANES)
                out_ref[at, :] = stencil_piece(
                    piece,
                    pieces,
                    lambda first, size: mid_ref[
                        pl.ds(pl.multiple_of(start + first, 16), size), :
                    ],
                    above_of(piece),
                    below_of(piece),
                    mix_wide[at, :],
                    stiff_wide[at, :],
                )

        def from_line(start):
            return lambda piece: mid_ref[
                pl.ds(pl.multiple_of(start + piece * LANES, LANES), LANES), :
            ]

        def from_halo(ref):
            return lambda piece: ref[piece * LANES : (piece + 1) * LANES, :]

        run(0, from_halo(low_ref), from_line(NY))

        @pl.loop(1, lines - 1)
        def _(line):
            start = pl.multiple_of(line * NY, NY)
            run(start, from_line(start - NY), from_line(start + NY))

        run((lines - 1) * NY, from_line((lines - 2) * NY), from_halo(high_ref))

    column = pl.BlockSpec((cells, LANES), lambda j: (0, j))
    halo = pl.BlockSpec((NY, LANES), lambda j: (0, j))
    coef = pl.BlockSpec((cells // LANES, LANES), lambda j: (0, 0))
    return pl.pallas_call(
        body,
        grid=(width // LANES,),
        in_specs=[column, coef, coef, halo, halo],
        out_specs=column,
        out_shape=jax.ShapeDtypeStruct((cells, width), BF16),
        scratch_shapes=[pltpu.VMEM((cells, LANES), F32)] * 2,
        compiler_params=pltpu.CompilerParams(vmem_limit_bytes=48 << 20),
        cost_estimate=pl.CostEstimate(
            flops=cells * width * 16, bytes_accessed=cells * width * 4, transcendentals=0
        ),
        name="full_field",
    )(sketch, mix, stiff, low, high)


def gram_lines(zfield, others, table, jobs):
    width = zfield.shape[1]
    total = sum(columns for _, columns, _ in others)

    def body(table_ref, z_ref, *rest):
        out_ref, acc_ref = rest[-2:]
        step = pl.program_id(0)
        parts = [ref[...] for ref in rest[:-2]]
        right = parts[0] if len(parts) == 1 else jnp.concatenate(parts, 1)
        product = lax.dot_general(right, z_ref[...], CELLS_FIRST, preferred_element_type=F32)

        @pl.when(step == 0)
        def _():
            acc_ref[...] = product

        @pl.when(step > 0)
        def _():
            acc_ref[...] += product

        @pl.when(step == jobs - 1)
        def _():
            out_ref[...] = jnp.transpose(acc_ref[...])

    return pl.pallas_call(
        body,
        grid_spec=pltpu.PrefetchScalarGridSpec(
            num_scalar_prefetch=1,
            grid=(jobs,),
            in_specs=[pl.BlockSpec((NY, width), lambda j, t: (t[0, j], 0))]
            + [pl.BlockSpec((NY, columns), block) for _, columns, block in others],
            out_specs=pl.BlockSpec((width, total), lambda j, t: (0, 0)),
            scratch_shapes=[pltpu.VMEM((total, width), F32)],
        ),
        out_shape=jax.ShapeDtypeStruct((width, total), F32),
        compiler_params=pltpu.CompilerParams(vmem_limit_bytes=32 << 20),
        cost_estimate=pl.CostEstimate(
            flops=2 * jobs * NY * width * total,
            bytes_accessed=jobs * NY * (width + total) * 2,
            transcendentals=0,
        ),
        name="gram_lines",
    )(table, zfield, *[array for array, _, _ in others])


def inverse_factor(block):
    def body(a_ref, o_ref):
        count = PB // 8
        sub = lax.broadcasted_iota(jnp.int32, (8, PB), 0)
        lane = lax.broadcasted_iota(jnp.int32, (8, PB), 1)
        left = [a_ref[8 * j : 8 * j + 8, :] for j in range(count)]
        right = [(lane == sub + 8 * j).astype(F32) for j in range(count)]
        for k in range(PB):
            top, s = divmod(k, 8)
            column = jnp.broadcast_to(left[top][:, k : k + 1], (8, PB))
            scale = lax.rsqrt(jnp.broadcast_to(column[s : s + 1, :], (8, PB)))
            row_left = jnp.broadcast_to(left[top][s : s + 1, :], (8, PB)) * scale
            row_right = jnp.broadcast_to(right[top][s : s + 1, :], (8, PB)) * scale
            for j in range(top, count):
                if j > top:
                    column = jnp.broadcast_to(left[j][:, k : k + 1], (8, PB))
                weight = column * scale
                if j == top:
                    weight = jnp.where(sub > s, weight, 0.0)
                left[j] = left[j] - weight * row_left
                right[j] = right[j] - weight * row_right
                if j == top:
                    right[j] = jnp.where(sub == s, row_right, right[j])
        for j in range(count):
            o_ref[8 * j : 8 * j + 8, :] = right[j]

    return pl.pallas_call(
        body,
        out_shape=jax.ShapeDtypeStruct((PB, PB), F32),
        cost_estimate=pl.CostEstimate(
            flops=40 << 20, bytes_accessed=PB * PB * 8, transcendentals=PB
        ),
        name="inverse_factor",
    )(block)


def finish(zfield, received, factor, solve_one, solve_cross, solve_two, table, pair):
    cells, width = zfield.shape
    lines = cells // NY
    rows = NY // 2
    per_line = NY // rows
    steps = lines * per_line
    half_steps = steps // 2

    def body(t, z_ref, r_ref, f_ref, one_ref, cross_ref, two_ref, res_ref, bas_ref, pan_ref):
        step = pl.program_id(0)
        role = t[0, 0]

        def tile(which):
            return z_ref[:, pl.ds(pl.multiple_of(t[0, which] * PB, PB), PB)]

        @pl.when(role == 0)
        def _():
            pan_ref[:, :PB] = tile(1)
            pan_ref[:, PB:] = tile(2) if pair else r_ref[...]

        @pl.when(role != 0)
        def _():
            if pair:
                pan_ref[...] = r_ref[...]
            else:
                pan_ref[:, :PB] = r_ref[...]
                pan_ref[:, PB:] = tile(1)

        one = lax.dot_general(
            pan_ref[:, :PB], one_ref[...], LAST_LAST, preferred_element_type=F32
        ).astype(BF16)
        partial = (
            pan_ref[:, PB:].astype(F32)
            - lax.dot_general(one, cross_ref[...], LAST_LAST, preferred_element_type=F32)
        ).astype(BF16)
        two = lax.dot_general(
            partial, two_ref[...], LAST_LAST, preferred_element_type=F32
        ).astype(BF16)
        both = jnp.concatenate([one, two], 1)

        @pl.when(step // half_steps == t[0, 3])
        def _():
            bas_ref[...] = both

        res_ref[...] = (
            z_ref[...].astype(F32)
            - lax.dot_general(both, f_ref[...], LAST_LAST, preferred_element_type=F32)
        ).astype(BF16)

    received_width = 2 * PB if pair else PB
    small = pl.BlockSpec((PB, PB), lambda j, t: (0, 0))
    line = pl.BlockSpec((rows, width), lambda j, t: (j, 0))
    return pl.pallas_call(
        body,
        grid_spec=pltpu.PrefetchScalarGridSpec(
            num_scalar_prefetch=1,
            grid=(steps,),
            in_specs=[
                line,
                pl.BlockSpec(
                    (rows, received_width),
                    lambda j, t: (
                        t[1, j // per_line] * per_line + j % per_line,
                        t[2, j // per_line],
                    ),
                ),
                pl.BlockSpec((width, 2 * PB), lambda j, t: (0, 0)),
                small,
                small,
                small,
            ],
            out_specs=[
                line,
                pl.BlockSpec(
                    (rows, 2 * PB),
                    lambda j, t: (jnp.clip(j - t[0, 3] * half_steps, 0, half_steps - 1), 0),
                ),
            ],
            scratch_shapes=[pltpu.VMEM((rows, 2 * PB), BF16)],
        ),
        out_shape=[
            jax.ShapeDtypeStruct((cells, width), BF16),
            jax.ShapeDtypeStruct((cells // 2, 2 * PB), BF16),
        ],
        compiler_params=pltpu.CompilerParams(vmem_limit_bytes=32 << 20),
        cost_estimate=pl.CostEstimate(
            flops=2 * cells * (2 * PB * width + 3 * PB * PB),
            bytes_accessed=cells * (4 * width + 3 * received_width + 2 * PB),
            transcendentals=0,
        ),
        name="finish",
    )(table, zfield, received, factor, solve_one, solve_cross, solve_two)


def swap(value):
    return lax.ppermute(value, "cols", SWAP)


def bit_of(bit):
    return lax.axis_index("rows") // bit % 2


def row_bits():
    count = lax.axis_size("rows")
    return [1 << k for k in range(count.bit_length() - 1)]


def over_rows(value, bit):
    count = lax.axis_size("rows")
    return lax.ppermute(value, "rows", [(k, k ^ bit) for k in range(count)])


def reduce_rows(split, whole=None):
    for bit in row_bits():
        half = split.shape[0] // 2
        side = bit_of(bit)
        keep = lax.dynamic_slice_in_dim(split, side * half, half, 0)
        send = lax.dynamic_slice_in_dim(split, (1 - side) * half, half, 0)
        if whole is None:
            split = keep + over_rows(send, bit)
        else:
            got = over_rows(jnp.concatenate([send, whole], 0), bit)
            split = keep + got[:half]
            whole = whole + got[half:]
    return split, whole


def slice_start(width):
    start = 0
    for bit in row_bits():
        width //= 2
        start = start + bit_of(bit) * width
    return start


def gather_rows(value):
    for bit in reversed(row_bits()):
        other = over_rows(value, bit)
        value = jnp.where(
            bit_of(bit) == 0,
            jnp.concatenate([value, other], 0),
            jnp.concatenate([other, value], 0),
        )
    return value


def dot_t(left, right):
    return lax.dot_general(left, right, LAST_LAST, precision=HIGHEST, preferred_element_type=F32)


def after(value, *events):
    return lax.optimization_barrier((value, *events))[0]


def two_groups(sketch, stiffness, reaction, panel_order):
    cells, width = sketch.shape
    lines = cells // NY
    panels_here = width // PB
    row_count = lax.axis_size("rows")
    scale = 1.0 / (cells * row_count)
    group = lax.axis_index("cols")
    first, second = panel_order[0], panel_order[1]
    group_one, group_two = first // panels_here, second // panels_here
    share = width // row_count
    eye = jnp.eye(PB, dtype=F32)

    def start(sketch, stiffness, reaction):
        stiff = stiffness.reshape(-1, LANES)
        mix = (reaction + 4.0 * stiffness).reshape(-1, LANES)
        forward = [(i, i + 1) for i in range(row_count - 1)]
        backward = [(i + 1, i) for i in range(row_count - 1)]
        low = lax.ppermute(sketch[cells - NY :], "rows", forward)
        high = lax.ppermute(sketch[:NY], "rows", backward)
        return mix, stiff, low, high

    def identity_rows(panel):
        position = group * width + slice_start(width) + jnp.arange(share, dtype=jnp.int32)
        offset = jnp.arange(PB, dtype=jnp.int32)
        return (position[:, None] == panel * PB + offset[None, :]).astype(F32)

    def end(zfield, received, one, two, inverse_one, cross, inverse_two, table, pair):
        core_one = one * scale + identity_rows(first)
        core_two = two * scale + identity_rows(second)
        column_one = dot_t(core_one, inverse_one)
        column_two = dot_t(core_two - dot_t(column_one, cross), inverse_two)
        factor = gather_rows(jnp.concatenate([column_one, column_two], 1))
        residual, basis = finish(
            zfield,
            received,
            factor.astype(BF16),
            inverse_one.astype(BF16),
            cross.astype(BF16),
            inverse_two.astype(BF16),
            table,
            pair,
        )
        return residual, basis, factor

    def apart(sketch, stiffness, reaction):
        mix, stiff, low, high = start(sketch, stiffness, reaction)
        holds_one = group == group_one
        role = jnp.where(holds_one, 0, 1).astype(jnp.int32)
        tile = (jnp.where(holds_one, first, second) % panels_here).astype(jnp.int32)
        orders = jnp.array([[1, 2, 3, 0, 4, 5, 6, 7], [4, 5, 6, 7, 1, 2, 3, 0]], jnp.int32)
        send, recv = orders[role], orders[1 - role]
        tiles = jnp.full((3,), tile, jnp.int32)
        early = panel_lines(sketch, mix, stiff, send[:3], tiles)
        got_early = swap(early)
        edge = panel_lines(sketch, mix, stiff, send[3:4], tiles[:1], low, high)
        got_edge = swap(edge)
        zfield = full_field(sketch, mix, stiff, low, high)

        def piece(slot):
            return lax.dynamic_slice(zfield, (send[slot] * NY, tile * PB), (NY, PB))

        late = jnp.concatenate([piece(4), piece(5), piece(6)], 1)
        got_late = swap(late)
        got_last = swap(piece(7))

        def table_of(*slots):
            return jnp.stack([jnp.stack([recv[s] for s in slots]), jnp.arange(len(slots))]).astype(
                jnp.int32
            )

        own_table = jnp.stack(
            [jnp.arange(lines, dtype=jnp.int32), jnp.full((lines,), tile, jnp.int32)]
        )
        own = gram_lines(
            zfield, [(zfield, PB, lambda j, t: (t[0, j], t[1, j]))], own_table, lines
        )
        side = lambda j, t: (0, t[1, j])
        half_one = gram_lines(zfield, [(got_early, PB, side)], table_of(0, 1, 2), 3) + gram_lines(
            zfield, [(got_edge, PB, side)], table_of(3), 1
        )
        own_rows = lambda value: lax.dynamic_slice_in_dim(value, tile * PB, PB, 0)
        own_share, whole = reduce_rows(
            own, jnp.concatenate([own_rows(own), own_rows(half_one)], 0)
        )
        diag_own, mixed_own = whole[:PB], whole[PB:]
        inverse_own = inverse_factor(diag_own * scale + eye)
        got = swap(jnp.concatenate([jnp.where(holds_one, inverse_own, diag_own), mixed_own], 0))
        mixed_other = got[PB:]
        inverse_one = jnp.where(holds_one, inverse_own, got[:PB])
        diag_two = jnp.where(holds_one, got[:PB], diag_own)
        mixed = jnp.where(holds_one, mixed_own.T + mixed_other, mixed_own + mixed_other.T)
        cross = dot_t(mixed * scale, inverse_one)
        inverse_two = inverse_factor(diag_two * scale + eye - dot_t(cross, cross))

        half_two = gram_lines(zfield, [(got_late, PB, side)], table_of(4, 5, 6), 3)
        rest = gram_lines(zfield, [(got_last, PB, side)], table_of(7), 1)
        other_share, _ = reduce_rows((half_one + half_two) + rest)
        one = jnp.where(holds_one, own_share, other_share)
        two = jnp.where(holds_one, other_share, own_share)
        received = jnp.concatenate([got_early, got_edge, got_late, got_last], 1)
        slots = jnp.zeros((lines,), jnp.int32).at[recv].set(jnp.arange(lines, dtype=jnp.int32))
        head = jnp.zeros((lines,), jnp.int32)
        head = head.at[0].set(role).at[1].set(tile).at[3].set(group)
        table = jnp.stack([head, jnp.zeros((lines,), jnp.int32), slots])
        return end(
            zfield, received, one, two, inverse_one, cross, inverse_two, table, False
        )

    def together(sketch, stiffness, reaction):
        mix, stiff, low, high = start(sketch, stiffness, reaction)
        owner = group == group_one
        tile_one = (first % panels_here).astype(jnp.int32)
        tile_two = (second % panels_here).astype(jnp.int32)
        count = width // LANES
        every = jnp.arange(count, dtype=jnp.int32)
        pairs = [(1, 2), (3, 4), (0, 7), (5, 6)]

        def jobs_for(pair, line):
            a, b = pair
            own_lines = jnp.array([a, a, b, b], jnp.int32)
            own_tiles = jnp.stack([tile_one, tile_two, tile_one, tile_two])
            return (
                jnp.where(owner, own_lines, jnp.full((count,), line, jnp.int32)),
                jnp.where(owner, own_tiles, every),
            )

        got = [swap(panel_lines(sketch, mix, stiff, *jobs_for(pairs[0], 5)))]
        got.append(swap(panel_lines(sketch, mix, stiff, *jobs_for(pairs[1], 6))))
        zfield = full_field(sketch, mix, stiff, low, high)

        def pieces(pair):
            return jnp.concatenate(
                [
                    lax.dynamic_slice(zfield, (line * NY, t * PB), (NY, PB))
                    for line in pair
                    for t in (tile_one, tile_two)
                ],
                1,
            )

        got.append(swap(pieces(pairs[2])))
        own_table = jnp.stack(
            [
                jnp.arange(lines, dtype=jnp.int32),
                jnp.full((lines,), tile_one, jnp.int32),
                jnp.full((lines,), tile_two, jnp.int32),
            ]
        )
        own = gram_lines(
            zfield,
            [
                (zfield, PB, lambda j, t: (t[0, j], t[1, j])),
                (zfield, PB, lambda j, t: (t[0, j], t[2, j])),
            ],
            own_table,
            lines,
        )
        own_share, whole = reduce_rows(
            own,
            jnp.concatenate(
                [lax.dynamic_slice_in_dim(own, t * PB, PB, 0) for t in (tile_one, tile_two)], 0
            ),
        )
        inverse_one = inverse_factor(whole[:PB, :PB] * scale + eye)
        cross = dot_t(whole[PB:, :PB] * scale, inverse_one)
        inverse_two = inverse_factor(whole[PB:, PB:] * scale + eye - dot_t(cross, cross))

        def owner_part(chunk, line):
            table = jnp.stack([jnp.array([0, 0, 0]), jnp.stack([line, tile_one, tile_two])])
            table = table.astype(jnp.int32)
            return gram_lines(
                chunk,
                [
                    (zfield, PB, lambda j, t: (t[1, 0], t[1, 1])),
                    (zfield, PB, lambda j, t: (t[1, 0], t[1, 2])),
                ],
                table,
                1,
            )

        def other_part(chunk, pair):
            table = jnp.array([pair, [0, 1]], jnp.int32)
            return gram_lines(chunk_field, [(chunk, 2 * PB, lambda j, t: (0, t[1, j]))], table, 2)

        chunk_field = zfield
        owner_sum = owner_part(got[0], jnp.int32(5)) + owner_part(got[1], jnp.int32(6))
        owner_share, _ = reduce_rows(owner_sum)
        small = jnp.concatenate(
            [
                inverse_one,
                cross,
                inverse_two,
                owner_share[:, :PB],
                owner_share[:, PB:],
            ],
            0,
        )
        got_small = swap(small)
        got.append(swap(after(pieces(pairs[3]), small)))
        inverse_one = jnp.where(owner, inverse_one, got_small[:PB])
        cross = jnp.where(owner, cross, got_small[PB : 2 * PB])
        inverse_two = jnp.where(owner, inverse_two, got_small[2 * PB : 3 * PB])
        extra = jnp.concatenate(
            [got_small[3 * PB : 3 * PB + share], got_small[3 * PB + share :]], 1
        )
        other_sum = (other_part(got[0], pairs[0]) + other_part(got[1], pairs[1])) + other_part(
            got[2], pairs[2]
        )
        other_share, _ = reduce_rows(other_sum)
        mine = jnp.where(owner, own_share, other_share + extra)
        received = jnp.concatenate(got, 0)
        head = jnp.zeros((lines,), jnp.int32)
        head = head.at[0].set(jnp.where(owner, 0, 1)).at[1].set(tile_one).at[2].set(tile_two)
        head = head.at[3].set(group)
        row_of, side_of = [0] * lines, [0] * lines
        for row, pair in enumerate(pairs):
            for side, line in enumerate(pair):
                row_of[line], side_of[line] = row, side
        table = jnp.stack(
            [head, jnp.array(row_of, jnp.int32), jnp.array(side_of, jnp.int32)]
        )
        return end(
            zfield,
            received,
            mine[:, :PB],
            mine[:, PB:],
            inverse_one,
            cross,
            inverse_two,
            table,
            True,
        )

    return lax.cond(group_one == group_two, together, apart, sketch, stiffness, reaction)


def per_device(sketch, stiffness, reaction, panel_order):
    cells, width = sketch.shape
    rows = lax.axis_size("rows")
    fits = lax.axis_size("cols") == 2 and cells == 8 * NY and width == 4 * PB
    if fits and rows & (rows - 1) == 0 and rows > 1:
        return two_groups(sketch, stiffness, reaction, panel_order)
    return any_groups(sketch, stiffness, reaction, panel_order)


def solution(mesh):
    return jax.shard_map(
        per_device,
        mesh=mesh,
        in_specs=(P("rows", "cols"), P("rows"), P("rows"), P()),
        out_specs=(P("rows", "cols"), P(("rows", "cols"), None), P("cols", None)),
        check_vma=False,
    )
```

```python
import jax
import jax.numpy as jnp
from jax import lax
from jax.experimental import pallas as pl
from jax.experimental.pallas import tpu as pltpu
from jax.sharding import PartitionSpec as P

PB = 128
NY = 2048
LANES = 128
BF16 = jnp.bfloat16
F32 = jnp.float32
HIGHEST = lax.Precision.HIGHEST
SWAP = [(0, 1), (1, 0)]
VMEM_BYTES = 56 << 20
LITTLE = pl.CostEstimate(flops=1 << 20, bytes_accessed=1 << 14, transcendentals=0)
CELLS_FIRST = (((0,), (0,)), ((), ()))
LAST_LAST = (((1,), (1,)), ((), ()))


def with_halo(block, sides, width):
    for axis, dim in sides:
        count = lax.axis_size(axis)
        forward = [(i, i + 1) for i in range(count - 1)]
        backward = [(target, source) for source, target in forward]
        low = lax.ppermute(
            lax.slice_in_dim(block, block.shape[dim] - width, None, axis=dim), axis, forward
        )
        high = lax.ppermute(lax.slice_in_dim(block, 0, width, axis=dim), axis, backward)
        block = jnp.concatenate([low, block, high], axis=dim)
    return block


def spread(value, axis, source):
    kept = jnp.where(lax.axis_index(axis) == source, value, 0).astype(value.dtype)
    return lax.psum(kept, axis)


def apply_operator(padded, cell_count, sketch, stiffness, reaction):
    centre = sketch.astype(jnp.float32)
    along_y = jnp.arange(cell_count) % NY
    upward = padded[:cell_count].astype(jnp.float32)
    downward = padded[2 * NY : 2 * NY + cell_count].astype(jnp.float32)
    leftward = jnp.where(
        (along_y == 0)[:, None], 0.0, padded[NY - 1 : NY - 1 + cell_count].astype(jnp.float32)
    )
    rightward = jnp.where(
        (along_y == NY - 1)[:, None], 0.0, padded[NY + 1 : NY + 1 + cell_count].astype(jnp.float32)
    )
    mixing = 4.0 * centre - upward - downward - leftward - rightward
    return (reaction[:, None] * centre + stiffness[:, None] * mixing).astype(jnp.bfloat16)


def factorize(gram_full, first_panel, second_panel, cell_total):
    width_all = gram_full.shape[0]
    positions = jnp.arange(width_all, dtype=jnp.int32)[:, None]
    offsets = jnp.arange(PB, dtype=jnp.int32)[None, :]
    ident_one = (positions == first_panel * PB + offsets).astype(jnp.float32)
    ident_two = (positions == second_panel * PB + offsets).astype(jnp.float32)
    core_block = gram_full / cell_total + jnp.concatenate([ident_one, ident_two], 1)
    diag_one = lax.dynamic_slice_in_dim(core_block[:, :PB], first_panel * PB, PB, 0)
    lower_one = jnp.linalg.cholesky(diag_one)
    identity = jnp.eye(PB, dtype=lower_one.dtype)
    inverse_one = jax.scipy.linalg.solve_triangular(lower_one, identity, lower=True)
    column_one = jnp.dot(core_block[:, :PB], inverse_one.T, precision=HIGHEST)
    cross_rows = lax.dynamic_slice_in_dim(column_one, second_panel * PB, PB, 0)
    updated = core_block[:, PB:] - jnp.dot(column_one, cross_rows.T, precision=HIGHEST)
    diag_two = lax.dynamic_slice_in_dim(updated, second_panel * PB, PB, 0)
    lower_two = jnp.linalg.cholesky(diag_two)
    inverse_two = jax.scipy.linalg.solve_triangular(lower_two, identity, lower=True)
    column_two = jnp.dot(updated, inverse_two.T, precision=HIGHEST)
    factor = jnp.concatenate([column_one, column_two], 1)
    return (factor, inverse_one, inverse_two, cross_rows)


def solve_basis(panel_one, panel_two, inverse_one, inverse_two, cross_rows):
    basis_one = jnp.dot(
        panel_one, inverse_one.T.astype(BF16), preferred_element_type=F32
    ).astype(BF16)
    partial_two = (
        panel_two.astype(F32)
        - jnp.dot(basis_one, cross_rows.T.astype(BF16), preferred_element_type=F32)
    ).astype(BF16)
    basis_two = jnp.dot(
        partial_two, inverse_two.T.astype(BF16), preferred_element_type=F32
    ).astype(BF16)
    return jnp.concatenate([basis_one, basis_two], 1)


def any_groups(sketch, stiffness, reaction, panel_order):
    cell_count, local_width = sketch.shape
    padded = with_halo(sketch, (("rows", 0),), NY)
    zfield = apply_operator(padded, cell_count, sketch, stiffness, reaction)
    groups = lax.axis_size("cols")
    own_group = lax.axis_index("cols")
    cell_total = cell_count * lax.axis_size("rows")
    first_panel = panel_order[0]
    second_panel = panel_order[1]
    slice_rows = cell_count // groups
    panels_here = local_width // PB

    def own_panel(panel_index):
        return lax.dynamic_slice_in_dim(zfield, panel_index % panels_here * PB, PB, 1)

    panel_one = spread(own_panel(first_panel), "cols", first_panel // panels_here)
    panel_two = spread(own_panel(second_panel), "cols", second_panel // panels_here)
    panels_both = jnp.concatenate([panel_one, panel_two], 1)
    partial_value = lax.dot_general(zfield, panels_both, CELLS_FIRST, preferred_element_type=F32)
    summed = lax.psum(partial_value, "rows")
    gram_full = lax.all_gather(summed, "cols", axis=0, tiled=True)
    factor, inverse_one, inverse_two, cross_rows = factorize(
        gram_full, first_panel, second_panel, cell_total
    )
    basis_full = solve_basis(panel_one, panel_two, inverse_one, inverse_two, cross_rows)
    own_factor = lax.dynamic_slice_in_dim(factor, own_group * local_width, local_width, 0).astype(
        BF16
    )
    residual = (
        zfield.astype(F32) - jnp.dot(basis_full, own_factor.T, preferred_element_type=F32)
    ).astype(BF16)
    basis_rows = lax.dynamic_slice_in_dim(basis_full, own_group * slice_rows, slice_rows, 0)
    factor_cols = lax.dynamic_slice_in_dim(factor, own_group * local_width, local_width, 0)
    return (residual, basis_rows, factor_cols)


def column_of(row):
    return jnp.transpose(jnp.broadcast_to(row, (LANES, LANES)))


WIDE = LANES + 32
PIECES = NY // LANES


def beside(lead):
    row = lax.broadcasted_iota(jnp.int32, (LANES, WIDE), 0) + lead
    col = lax.broadcasted_iota(jnp.int32, (LANES, WIDE), 1)
    return jnp.where((col == row - 1) | (col == row + 1), 1.0, 0.0).astype(BF16)


def stencil_piece(number, load, above, below, mix_col, stiff_col):
    lead = 0 if number == 0 else 32 if number == PIECES - 1 else 16
    wide = load(number * LANES - lead, WIDE)
    sides = jnp.dot(beside(lead), wide, preferred_element_type=F32)
    around = (above.astype(F32) + below.astype(F32)) + sides
    centre = load(number * LANES, LANES).astype(F32)
    return (mix_col * centre - stiff_col * around).astype(BF16)


def panel_lines(sketch, mix, stiff, info, jobs, line_of, tile_of, low=None, high=None):
    last_line = sketch.shape[0] // NY - 1

    def body(info_ref, up_ref, mid_ref, down_ref, mix_ref, stiff_ref, *rest):
        out_ref = rest[-1]

        def run(above, below):
            for number in range(PIECES):
                at = slice(number * LANES, (number + 1) * LANES)
                out_ref[at, :] = stencil_piece(
                    number,
                    lambda start, size: mid_ref[start : start + size, :],
                    above[at, :],
                    below[at, :],
                    column_of(mix_ref[number : number + 1, :]),
                    column_of(stiff_ref[number : number + 1, :]),
                )

        if low is None:
            run(up_ref, down_ref)
        else:
            line = line_of(pl.program_id(0), info_ref)

            @pl.when(line == 0)
            def _():
                run(rest[0], down_ref)

            @pl.when(line == last_line)
            def _():
                run(up_ref, rest[1])

    def block(shift):
        return pl.BlockSpec(
            (NY, LANES),
            lambda j, t: (jnp.clip(line_of(j, t) + shift, 0, last_line), tile_of(j, t)),
        )

    coef = pl.BlockSpec((PIECES, LANES), lambda j, t: (line_of(j, t), 0))
    halo = pl.BlockSpec((NY, LANES), lambda j, t: (0, 0))
    extra = [] if low is None else [low, high]
    return pl.pallas_call(
        body,
        grid_spec=pltpu.PrefetchScalarGridSpec(
            num_scalar_prefetch=1,
            grid=(jobs,),
            in_specs=[block(-1), block(0), block(1), coef, coef] + [halo] * len(extra),
            out_specs=pl.BlockSpec((NY, LANES), lambda j, t: (0, j)),
        ),
        out_shape=jax.ShapeDtypeStruct((NY, jobs * LANES), BF16),
        compiler_params=pltpu.CompilerParams(vmem_limit_bytes=VMEM_BYTES),
        cost_estimate=LITTLE,
        name="panel_lines",
    )(info, sketch, sketch, sketch, mix, stiff, *extra)


def field_part(sketch, mix, stiff, info, panels, jobs, stride, line_of, sources, base=None):
    cells, width = sketch.shape
    arrays = []
    for copies in sources:
        for array, *_ in copies:
            if not any(array is known for known in arrays):
                arrays.append(array)
    index = lambda array: [array is known for known in arrays].index(True)
    plan = [
        (slot, index(array), row, column, size, place)
        for slot, copies in enumerate(sources)
        for array, row, column, size, place in copies
    ]

    def body(info_ref, *refs):
        hbm, rest = refs[: len(arrays)], refs[len(arrays) :]
        mix_ref, stiff_ref = rest[:2]
        z_ref, gram_ref, lines_ref, acc_ref, sems = rest[-5:]
        step = pl.program_id(0)

        def copy_of(number):
            slot, which, row, column, size, place = plan[number]
            at = place(info_ref)
            at = at if isinstance(at, int) else pl.multiple_of(at, LANES)
            return pltpu.make_async_copy(
                hbm[which].at[row : row + NY, column : column + size],
                lines_ref.at[slot, :, pl.ds(at, size)],
                sems.at[number],
            )

        def wait_for(slots):
            for number, entry in enumerate(plan):
                if entry[0] in slots:
                    copy_of(number).wait()

        @pl.when(step == 0)
        def _():
            for number in range(len(plan)):
                copy_of(number).start()
            wait_for((0, 1, 2))

        for job in range(1, jobs):

            @pl.when(step == job)
            def _():
                wait_for([stride * job + k for k in range(3) if k >= 3 - stride])

        first = step * stride
        for number in range(PIECES):
            at = slice(number * LANES, (number + 1) * LANES)
            mix_col = column_of(mix_ref[number : number + 1, :])
            stiff_col = column_of(stiff_ref[number : number + 1, :])
            for tile in range(width // LANES):
                cols = slice(tile * LANES, (tile + 1) * LANES)
                z_ref[at, cols] = stencil_piece(
                    number,
                    lambda start, size: lines_ref[first + 1, start : start + size, cols],
                    lines_ref[first, at, cols],
                    lines_ref[first + 2, at, cols],
                    mix_col,
                    stiff_col,
                )

        own = [
            z_ref[:, pl.ds(pl.multiple_of(info_ref[1 + k] * PB, PB), PB)] for k in range(panels)
        ]
        own = own[0] if panels == 1 else jnp.concatenate(own, 1)
        product = lax.dot_general(own, z_ref[...], CELLS_FIRST, preferred_element_type=F32)

        @pl.when(step == 0)
        def _():
            acc_ref[...] = product

        @pl.when(step > 0)
        def _():
            acc_ref[...] += product

        @pl.when(step == jobs - 1)
        def _():
            gram_ref[...] = jnp.transpose(acc_ref[...])

    coef = pl.BlockSpec((PIECES, LANES), lambda j, t: (line_of(j, t), 0))
    ANY = pl.BlockSpec(memory_space=pl.ANY)
    extra = [] if base is None else [base]
    return pl.pallas_call(
        body,
        grid_spec=pltpu.PrefetchScalarGridSpec(
            num_scalar_prefetch=1,
            grid=(jobs,),
            in_specs=[ANY] * len(arrays) + [coef, coef] + [ANY] * len(extra),
            out_specs=[
                pl.BlockSpec((NY, width), lambda j, t: (line_of(j, t), 0)),
                pl.BlockSpec((width, panels * PB), lambda j, t: (0, 0)),
            ],
            scratch_shapes=[
                pltpu.VMEM((len(sources), NY, width), BF16),
                pltpu.VMEM((panels * PB, width), F32),
                pltpu.SemaphoreType.DMA((len(plan),)),
            ],
        ),
        out_shape=[
            jax.ShapeDtypeStruct((cells, width), BF16),
            jax.ShapeDtypeStruct((width, panels * PB), F32),
        ],
        input_output_aliases={} if base is None else {3 + len(arrays): 0},
        compiler_params=pltpu.CompilerParams(vmem_limit_bytes=VMEM_BYTES),
        cost_estimate=LITTLE,
        name="field_part",
    )(info, *arrays, mix, stiff, *extra)


def whole_field(sketch, mix, stiff, info, panels, low, high):
    width = sketch.shape[1]
    lines = sketch.shape[0] // NY

    def line(number):
        return [(sketch, number * NY, 0, width, lambda t: 0)]

    field, gram = field_part(
        sketch,
        mix,
        stiff,
        info,
        panels,
        lines - 2,
        1,
        lambda j, t: j + 1,
        [line(k) for k in range(lines)],
    )
    field, more = field_part(
        sketch,
        mix,
        stiff,
        info,
        panels,
        2,
        3,
        lambda j, t: j * (lines - 1),
        [low, line(0), line(1), line(lines - 2), line(lines - 1), high],
        field,
    )
    return field, gram + more


def copy_lines(source, info, jobs, line_of, tile_of, width=LANES):
    def body(info_ref, z_ref, out_ref):
        out_ref[...] = z_ref[...]

    return pl.pallas_call(
        body,
        grid_spec=pltpu.PrefetchScalarGridSpec(
            num_scalar_prefetch=1,
            grid=(jobs,),
            in_specs=[pl.BlockSpec((NY, width), lambda j, t: (line_of(j, t), tile_of(j, t)))],
            out_specs=pl.BlockSpec((NY, width), lambda j, t: (0, j)),
        ),
        out_shape=jax.ShapeDtypeStruct((NY, jobs * width), BF16),
        compiler_params=pltpu.CompilerParams(vmem_limit_bytes=VMEM_BYTES),
        cost_estimate=LITTLE,
        name="copy_lines",
    )(info, source)


def gram_lines(zfield, others, info, jobs, line_of):
    width = zfield.shape[1]
    total = sum(columns for _, columns, _ in others)

    def body(info_ref, z_ref, *rest):
        out_ref, acc_ref = rest[-2:]
        step = pl.program_id(0)
        parts = [ref[...] for ref in rest[:-2]]
        right = parts[0] if len(parts) == 1 else jnp.concatenate(parts, 1)
        product = lax.dot_general(right, z_ref[...], CELLS_FIRST, preferred_element_type=F32)

        @pl.when(step == 0)
        def _():
            acc_ref[...] = product

        @pl.when(step > 0)
        def _():
            acc_ref[...] += product

        @pl.when(step == jobs - 1)
        def _():
            out_ref[...] = jnp.transpose(acc_ref[...])

    return pl.pallas_call(
        body,
        grid_spec=pltpu.PrefetchScalarGridSpec(
            num_scalar_prefetch=1,
            grid=(jobs,),
            in_specs=[pl.BlockSpec((NY, width), lambda j, t: (line_of(j, t), 0))]
            + [pl.BlockSpec((NY, columns), block) for _, columns, block in others],
            out_specs=pl.BlockSpec((width, total), lambda j, t: (0, 0)),
            scratch_shapes=[pltpu.VMEM((total, width), F32)],
        ),
        out_shape=jax.ShapeDtypeStruct((width, total), F32),
        compiler_params=pltpu.CompilerParams(vmem_limit_bytes=VMEM_BYTES),
        cost_estimate=LITTLE,
        name="gram_lines",
    )(info, zfield, *[array for array, _, _ in others])


def inverse_factor(block):
    def body(a_ref, o_ref, work):
        sub = lax.broadcasted_iota(jnp.int32, (8, PB), 0)
        row = lax.broadcasted_iota(jnp.int32, (PB, PB), 0)
        lane = lax.broadcasted_iota(jnp.int32, (PB, PB), 1)
        work[:, :PB] = a_ref[...]
        work[:, PB:] = (row == lane).astype(F32)

        def spread_row(value, s):
            return jnp.broadcast_to(value[s : s + 1, :], (8, PB))

        @pl.loop(0, PB // 8)
        def _(step):
            at = pl.ds(pl.multiple_of(step * 8, 8), 8)
            left, right = work[at, :PB], work[at, PB:]
            near = pltpu.roll(left, (PB - step * 8) % PB, 1)
            columns = [jnp.broadcast_to(near[:, c : c + 1], (8, PB)) for c in range(8)]
            for s in range(8):
                scale = lax.rsqrt(spread_row(columns[s], s))
                row_left = spread_row(left, s) * scale
                row_right = spread_row(right, s) * scale
                weight = jnp.where(sub > s, columns[s] * scale, 0.0)
                left = jnp.where(sub == s, row_left, left - weight * row_left)
                right = jnp.where(sub == s, row_right, right - weight * row_right)
                for c in range(s + 1, 8):
                    columns[c] = columns[c] - weight * (spread_row(columns[s], c) * scale)
            o_ref[at, :] = right
            both = jnp.concatenate([left, right], 1)
            work[...] -= lax.dot_general(
                left, both, CELLS_FIRST, precision=HIGHEST, preferred_element_type=F32
            )

    return pl.pallas_call(
        body,
        out_shape=jax.ShapeDtypeStruct((PB, PB), F32),
        scratch_shapes=[pltpu.VMEM((PB, 2 * PB), F32)],
        cost_estimate=LITTLE,
        name="inverse_factor",
    )(block)


def finish(zfield, chunks, solves, factor, info, pair, slot_of):
    cells, width = zfield.shape
    lines = cells // NY
    block = 2 * PB if pair else PB
    arrays = []
    for array, _ in chunks:
        if not any(array is known for known in arrays):
            arrays.append(array)
    index = lambda array: [array is known for known in arrays].index(True)

    def body(t, *refs):
        hbm, rest = refs[: len(arrays)], refs[len(arrays) :]
        z_ref, one_ref, cross_ref, two_ref, f_ref, out_ref, half_ref = rest[:7]
        got_ref, pan_ref, bas_ref, sems = rest[7:]
        step = pl.program_id(0)
        role = t[0]

        def copy_of(slot):
            array, column = chunks[slot]
            return pltpu.make_async_copy(
                hbm[index(array)].at[:, column : column + block], got_ref.at[slot], sems.at[slot]
            )

        @pl.when(step == 0)
        def _():
            for slot in range(lines):
                copy_of(slot).start()

        mine = slot_of(step, t)
        for slot in range(lines):

            @pl.when(mine == slot)
            def _():
                copy_of(slot).wait()

        def tile(which):
            return z_ref[:, pl.ds(pl.multiple_of(t[which] * PB, PB), PB)]

        @pl.when(role == 0)
        def _():
            pan_ref[:, :PB] = tile(1)
            pan_ref[:, PB:] = tile(2) if pair else got_ref[mine]

        @pl.when(role != 0)
        def _():
            if pair:
                pan_ref[...] = got_ref[mine]
            else:
                pan_ref[:, :PB] = got_ref[mine]
                pan_ref[:, PB:] = tile(1)

        one = lax.dot_general(
            pan_ref[:, :PB], one_ref[...], LAST_LAST, preferred_element_type=F32
        ).astype(BF16)
        partial = (
            pan_ref[:, PB:].astype(F32)
            - lax.dot_general(one, cross_ref[...], LAST_LAST, preferred_element_type=F32)
        ).astype(BF16)
        two = lax.dot_general(
            partial, two_ref[...], LAST_LAST, preferred_element_type=F32
        ).astype(BF16)
        bas_ref[:, :PB] = one
        bas_ref[:, PB:] = two
        out_ref[...] = (
            z_ref[...].astype(F32)
            - lax.dot_general(
                bas_ref[...], f_ref[...], LAST_LAST, preferred_element_type=F32
            )
        ).astype(BF16)

        @pl.when(step // (lines // 2) == t[3])
        def _():
            half_ref[...] = bas_ref[...]

    small = pl.BlockSpec((PB, PB), lambda j, t: (0, 0))
    line = pl.BlockSpec((NY, width), lambda j, t: (j, 0))
    last = lines // 2 - 1
    return pl.pallas_call(
        body,
        grid_spec=pltpu.PrefetchScalarGridSpec(
            num_scalar_prefetch=1,
            grid=(lines,),
            in_specs=[pl.BlockSpec(memory_space=pl.ANY)] * len(arrays)
            + [line, small, small, small, pl.BlockSpec((width, 2 * PB), lambda j, t: (0, 0))],
            out_specs=[
                line,
                pl.BlockSpec(
                    (NY, 2 * PB), lambda j, t: (jnp.clip(j - t[3] * (last + 1), 0, last), 0)
                ),
            ],
            scratch_shapes=[
                pltpu.VMEM((lines, NY, block), BF16),
                pltpu.VMEM((NY, 2 * PB), BF16),
                pltpu.VMEM((NY, 2 * PB), BF16),
                pltpu.SemaphoreType.DMA((lines,)),
            ],
        ),
        out_shape=[
            jax.ShapeDtypeStruct((cells, width), BF16),
            jax.ShapeDtypeStruct((cells // 2, 2 * PB), BF16),
        ],
        compiler_params=pltpu.CompilerParams(vmem_limit_bytes=VMEM_BYTES),
        cost_estimate=LITTLE,
        name="finish",
    )(info, *arrays, zfield, *solves, factor)


def swap(value):
    return lax.ppermute(value, "cols", SWAP)


def bit_of(bit):
    return lax.axis_index("rows") // bit % 2


def row_bits():
    count = lax.axis_size("rows")
    return [1 << k for k in range(count.bit_length() - 1)]


def over_rows(value, bit):
    count = lax.axis_size("rows")
    return lax.ppermute(value, "rows", [(k, k ^ bit) for k in range(count)])


def sum_rows(value):
    for bit in row_bits():
        value = value + over_rows(value, bit)
    return value


def reduce_rows(split, whole=None):
    for bit in row_bits():
        half = split.shape[0] // 2
        side = bit_of(bit)
        keep = lax.dynamic_slice_in_dim(split, side * half, half, 0)
        send = lax.dynamic_slice_in_dim(split, (1 - side) * half, half, 0)
        if whole is None:
            split = keep + over_rows(send, bit)
        else:
            got = over_rows(jnp.concatenate([send, whole], 0), bit)
            split = keep + got[:half]
            whole = whole + got[half:]
    return split, whole


def slice_start(width):
    start = 0
    for bit in row_bits():
        width //= 2
        start = start + bit_of(bit) * width
    return start


def gather_rows(value):
    for bit in reversed(row_bits()):
        other = over_rows(value, bit)
        value = jnp.where(
            bit_of(bit) == 0,
            jnp.concatenate([value, other], 0),
            jnp.concatenate([other, value], 0),
        )
    return value


def dot_t(left, right):
    return lax.dot_general(left, right, LAST_LAST, precision=HIGHEST, preferred_element_type=F32)


def step_of(live, work, *values):
    shapes = jax.eval_shape(work, *values)
    empty = lambda *_: jax.tree.map(lambda shape: jnp.zeros(shape.shape, shape.dtype), shapes)
    return lax.cond(live, work, empty, *values)


def after(value, *events):
    return lax.optimization_barrier((value, *events))[0]


def two_groups(sketch, stiffness, reaction, panel_order):
    cells, width = sketch.shape
    lines = cells // NY
    panels_here = width // PB
    row_count = lax.axis_size("rows")
    scale = 1.0 / (cells * row_count)
    group = lax.axis_index("cols")
    first, second = panel_order[0], panel_order[1]
    group_one, group_two = first // panels_here, second // panels_here
    share = width // row_count
    eye = jnp.eye(PB, dtype=F32)
    tile_one = first % panels_here
    tile_two = second % panels_here
    holds_one = group == group_one
    role = jnp.where(holds_one, 0, 1)

    def upward(value):
        return lax.ppermute(value, "rows", [(i, i + 1) for i in range(row_count - 1)])

    def downward(value):
        return lax.ppermute(value, "rows", [(i + 1, i) for i in range(row_count - 1)])

    def identity_rows(panel):
        position = group * width + slice_start(width) + jnp.arange(share, dtype=jnp.int32)
        offset = jnp.arange(PB, dtype=jnp.int32)
        return (position[:, None] == panel * PB + offset[None, :]).astype(F32)

    def factor_of(one, two, inverse_one, cross, inverse_two):
        core_one = one * scale + identity_rows(first)
        core_two = two * scale + identity_rows(second)
        column_one = dot_t(core_one, inverse_one)
        column_two = dot_t(core_two - dot_t(column_one, cross), inverse_two)
        return gather_rows(jnp.concatenate([column_one, column_two], 1))

    def apart(sketch, mix, stiff, info):
        def order(slot, turned):
            turned = jnp.asarray(turned, jnp.int32)
            near = (slot + 1) & 3
            return jnp.where((slot < 4) == (turned == 0), near, (slot & 3) + 4)

        def sent(slot):
            return lambda j, t: order(slot + j, t[0])

        def came(slot):
            return lambda j, t: order(slot + j, 1 - t[0])

        own_tile = lambda j, t: t[1]
        tile_after = lambda j, t: (t[1] + 1 + j) % panels_here
        bottom, top = lambda j, t: lines - 1, lambda j, t: 0
        early = panel_lines(sketch, mix, stiff, info, 3, sent(0), own_tile)
        got_early = swap(early)
        others = panels_here - 1

        def own_halo(sketch, info):
            low = upward(copy_lines(sketch, info, 1, bottom, own_tile))
            return low, downward(copy_lines(sketch, info, 1, top, own_tile))

        live = info[3] >= 0
        low_own, high_own = step_of(live, own_halo, after(sketch, early), info)
        late = panel_lines(sketch, mix, stiff, info, 3, sent(4), own_tile)
        edges = panel_lines(
            sketch,
            mix,
            stiff,
            info,
            2,
            lambda j, t: order(3 + 4 * j, t[0]),
            own_tile,
            low_own,
            high_own,
        )
        edge, last = edges[:, :PB], edges[:, PB:]
        got_edge = swap(edge)
        got_late = swap(after(late, edge))
        got_last = swap(after(last, late, edge))

        def halo_copies(own, rest):
            copies = [(own, 0, 0, PB, lambda t: t[1] * PB)]
            for j in range(others):
                copies.append((rest, 0, j * PB, PB, lambda t, j=j: tile_after(j, t) * PB))
            return copies

        def local_field(sketch, mix, stiff, info, low_own, high_own):
            low_rest = upward(copy_lines(sketch, info, others, bottom, tile_after))
            high_rest = downward(copy_lines(sketch, info, others, top, tile_after))
            low, high = halo_copies(low_own, low_rest), halo_copies(high_own, high_rest)
            return whole_field(sketch, mix, stiff, info, 1, low, high)

        zfield, own = step_of(
            live, local_field, after(sketch, late, edges), mix, stiff, info, low_own, high_own
        )
        side = lambda j, t: (0, j)
        half_one = gram_lines(
            zfield, [(got_early, PB, side)], info, 3, came(0)
        ) + gram_lines(zfield, [(got_edge, PB, side)], info, 1, came(3))

        def first_sums(own, half_one, info):
            own_rows = lambda value: lax.dynamic_slice_in_dim(value, info[1] * PB, PB, 0)
            own_share, whole = reduce_rows(
                own, jnp.concatenate([own_rows(own), own_rows(half_one)], 0)
            )
            return own_share, whole, inverse_factor(whole[:PB] * scale + eye)

        own_share, whole, inverse_own = step_of(live, first_sums, own, half_one, info)
        diag_own, mixed_own = whole[:PB], whole[PB:]
        small = jnp.concatenate([jnp.where(holds_one, inverse_own, diag_own), mixed_own], 0)
        got_small = swap(small)
        half_two = gram_lines(zfield, [(after(got_late, whole), PB, side)], info, 3, came(4))
        mixed_other = got_small[PB:]
        inverse_one = jnp.where(holds_one, inverse_own, got_small[:PB])
        diag_two = jnp.where(holds_one, got_small[:PB], diag_own)
        mixed = jnp.where(holds_one, mixed_own.T + mixed_other, mixed_own + mixed_other.T)
        rest = gram_lines(zfield, [(after(got_last, whole), PB, side)], info, 1, came(7))

        def last_sums(other, own_share, inverse_one, diag_two, mixed):
            cross = dot_t(mixed * scale, inverse_one)
            inverse_two = inverse_factor(diag_two * scale + eye - dot_t(cross, cross))
            other_share, _ = reduce_rows(other)
            one = jnp.where(holds_one, own_share, other_share)
            two = jnp.where(holds_one, other_share, own_share)
            factor = factor_of(one, two, inverse_one, cross, inverse_two)
            return factor, cross, inverse_two

        factor, cross, inverse_two = step_of(
            live,
            last_sums,
            (half_one + half_two) + rest,
            own_share,
            inverse_one,
            diag_two,
            mixed,
        )

        def slot_of(line, t):
            near = (line + 3) & 3
            return jnp.where(
                t[0] == 0, jnp.where(line < 4, near + 4, line - 4), jnp.where(line < 4, near, line)
            )

        solves = [value.astype(BF16) for value in (inverse_one, cross, inverse_two)]
        chunks = [(got_early, 0), (got_early, PB), (got_early, 2 * PB), (got_edge, 0)]
        chunks += [(got_late, 0), (got_late, PB), (got_late, 2 * PB), (got_last, 0)]
        residual, basis_rows = finish(
            zfield, chunks, solves, factor.astype(BF16), info, False, slot_of
        )
        return residual, basis_rows, factor

    def together(sketch, mix, stiff, info):
        owner = holds_one
        pairs = [(1, 2), (3, 4), (0, 7), (5, 6)]

        def tile_at(j, t):
            return jnp.where(j % 2 == 0, t[1], t[2])

        def chunk(near, far):
            return panel_lines(
                sketch,
                mix,
                stiff,
                info,
                4,
                lambda j, t: jnp.where(t[0] == 0, near + j // 2, far),
                lambda j, t: jnp.where(t[0] == 0, tile_at(j, t), j),
            )

        chunk_one = chunk(1, 5)
        got_one = swap(chunk_one)
        chunk_two = chunk(3, 6)
        got_two = swap(chunk_two)
        live = info[3] >= 0
        nothing = lambda j, t: 0
        whole_line = lambda halo: [(halo, 0, 0, width, lambda t: 0)]

        def local_field(sketch, mix, stiff, info):
            low = upward(copy_lines(sketch, info, 1, lambda j, t: lines - 1, nothing, width))
            high = downward(copy_lines(sketch, info, 1, nothing, nothing, width))
            zfield, own = whole_field(
                sketch, mix, stiff, info, 2, whole_line(low), whole_line(high)
            )
            chunks = [copy_lines(zfield, info, 4, lambda j, t: j // 2 * 7, tile_at)]
            for line in (5, 6):
                chunks.append(copy_lines(zfield, info, 2, lambda j, t, k=line: k, tile_at))
            return zfield, own, *chunks

        sketch = after(sketch, chunk_one, chunk_two)
        zfield, own, chunk_three, chunk_four, chunk_five = step_of(
            live, local_field, sketch, mix, stiff, info
        )
        got_three = swap(chunk_three)
        got_four = swap(after(chunk_four, chunk_three))

        def own_sums(own, info):
            own_share, _ = reduce_rows(own)
            total = gather_rows(own_share)
            whole = jnp.concatenate(
                [lax.dynamic_slice_in_dim(total, info[k] * PB, PB, 0) for k in (1, 2)], 0
            )
            inverse_one = inverse_factor(whole[:PB, :PB] * scale + eye)
            cross = dot_t(whole[PB:, :PB] * scale, inverse_one)
            schur = whole[PB:, PB:] * scale + eye - dot_t(cross, cross)
            return own_share, inverse_one, cross, inverse_factor(schur)

        own_share, inverse_one, cross, inverse_two = step_of(
            live, own_sums, after(own, chunk_three), info
        )

        def owner_part(received, line):
            return gram_lines(
                received,
                [
                    (zfield, PB, lambda j, t: (line, t[1])),
                    (zfield, PB, lambda j, t: (line, t[2])),
                ],
                info,
                1,
                lambda j, t: 0,
            )

        def other_part(received, pair):
            return gram_lines(
                zfield,
                [(received, 2 * PB, lambda j, t: (0, j))],
                info,
                2,
                lambda j, t: pair[0] + j * (pair[1] - pair[0]),
            )

        late_two = after(got_two, inverse_two)
        owner_share = step_of(
            live,
            lambda part: reduce_rows(part)[0],
            owner_part(got_one, 5) + owner_part(late_two, 6),
        )
        small = jnp.concatenate(
            [inverse_one, cross, inverse_two, owner_share[:, :PB], owner_share[:, PB:]], 0
        )
        got_small = swap(small)
        got_five = swap(after(chunk_five, got_small))
        late_three = after(got_three, small)
        inverse_one = jnp.where(owner, inverse_one, got_small[:PB])
        cross = jnp.where(owner, cross, got_small[PB : 2 * PB])
        inverse_two = jnp.where(owner, inverse_two, got_small[2 * PB : 3 * PB])
        extra = jnp.concatenate(
            [got_small[3 * PB : 3 * PB + share], got_small[3 * PB + share :]], 1
        )
        other_sum = (other_part(got_one, pairs[0]) + other_part(late_two, pairs[1])) + other_part(
            late_three, pairs[2]
        )

        def last_sums(other_sum, own_share, extra, inverse_one, cross, inverse_two):
            other_share, _ = reduce_rows(other_sum)
            mine = jnp.where(owner, own_share, other_share + extra)
            return factor_of(mine[:, :PB], mine[:, PB:], inverse_one, cross, inverse_two)

        factor = step_of(
            live, last_sums, other_sum, own_share, extra, inverse_one, cross, inverse_two
        )

        def slot_of(line, t):
            return jnp.where(line == 0, 4, jnp.where(line == 7, 5, jnp.where(line < 5, line - 1, line + 1)))

        solves = [value.astype(BF16) for value in (inverse_one, cross, inverse_two)]
        chunks = [
            (array, column) for array in (got_one, got_two, got_three) for column in (0, 2 * PB)
        ]
        chunks += [(got_four, 0), (after(got_five, factor), 0)]
        residual, basis_rows = finish(
            zfield, chunks, solves, factor.astype(BF16), info, True, slot_of
        )
        return residual, basis_rows, factor

    stiff = stiffness.reshape(-1, LANES)
    mix = (reaction + 4.0 * stiffness).reshape(-1, LANES)
    same = group_one == group_two
    info = jnp.stack(
        [
            role,
            jnp.where(same | holds_one, tile_one, tile_two),
            jnp.where(same | (role == 1), tile_two, tile_one),
            group,
        ]
    ).astype(jnp.int32)
    return lax.cond(same, together, apart, sketch, mix, stiff, info)


def per_device(sketch, stiffness, reaction, panel_order):
    cells, width = sketch.shape
    rows = lax.axis_size("rows")
    fits = lax.axis_size("cols") == 2 and cells == 8 * NY and width == 4 * PB
    if fits and rows & (rows - 1) == 0 and rows > 1:
        return two_groups(sketch, stiffness, reaction, panel_order)
    return any_groups(sketch, stiffness, reaction, panel_order)


def solution(mesh):
    return jax.shard_map(
        per_device,
        mesh=mesh,
        in_specs=(P("rows", "cols"), P("rows"), P("rows"), P()),
        out_specs=(P("rows", "cols"), P(("rows", "cols"), None), P("cols", None)),
        check_vma=False,
    )
```

```python
import jax
import jax.numpy as jnp
from jax import lax
from jax.experimental import pallas as pl
from jax.experimental.pallas import tpu as pltpu
from jax.sharding import PartitionSpec as P

PB = 128
NY = 2048
LANES = 128
BF16 = jnp.bfloat16
F32 = jnp.float32
HIGHEST = lax.Precision.HIGHEST
SWAP = [(0, 1), (1, 0)]
VMEM_BYTES = 56 << 20
LITTLE = pl.CostEstimate(flops=1 << 20, bytes_accessed=1 << 14, transcendentals=0)
CELLS_FIRST = (((0,), (0,)), ((), ()))
LAST_LAST = (((1,), (1,)), ((), ()))


def with_halo(block, sides, width):
    for axis, dim in sides:
        count = lax.axis_size(axis)
        forward = [(i, i + 1) for i in range(count - 1)]
        backward = [(target, source) for source, target in forward]
        low = lax.ppermute(
            lax.slice_in_dim(block, block.shape[dim] - width, None, axis=dim), axis, forward
        )
        high = lax.ppermute(lax.slice_in_dim(block, 0, width, axis=dim), axis, backward)
        block = jnp.concatenate([low, block, high], axis=dim)
    return block


def spread(value, axis, source):
    kept = jnp.where(lax.axis_index(axis) == source, value, 0).astype(value.dtype)
    return lax.psum(kept, axis)


def apply_operator(padded, cell_count, sketch, stiffness, reaction):
    centre = sketch.astype(jnp.float32)
    along_y = jnp.arange(cell_count) % NY
    upward = padded[:cell_count].astype(jnp.float32)
    downward = padded[2 * NY : 2 * NY + cell_count].astype(jnp.float32)
    leftward = jnp.where(
        (along_y == 0)[:, None], 0.0, padded[NY - 1 : NY - 1 + cell_count].astype(jnp.float32)
    )
    rightward = jnp.where(
        (along_y == NY - 1)[:, None], 0.0, padded[NY + 1 : NY + 1 + cell_count].astype(jnp.float32)
    )
    mixing = 4.0 * centre - upward - downward - leftward - rightward
    return (reaction[:, None] * centre + stiffness[:, None] * mixing).astype(jnp.bfloat16)


def factorize(gram_full, first_panel, second_panel, cell_total):
    width_all = gram_full.shape[0]
    positions = jnp.arange(width_all, dtype=jnp.int32)[:, None]
    offsets = jnp.arange(PB, dtype=jnp.int32)[None, :]
    ident_one = (positions == first_panel * PB + offsets).astype(jnp.float32)
    ident_two = (positions == second_panel * PB + offsets).astype(jnp.float32)
    core_block = gram_full / cell_total + jnp.concatenate([ident_one, ident_two], 1)
    diag_one = lax.dynamic_slice_in_dim(core_block[:, :PB], first_panel * PB, PB, 0)
    lower_one = jnp.linalg.cholesky(diag_one)
    identity = jnp.eye(PB, dtype=lower_one.dtype)
    inverse_one = jax.scipy.linalg.solve_triangular(lower_one, identity, lower=True)
    column_one = jnp.dot(core_block[:, :PB], inverse_one.T, precision=HIGHEST)
    cross_rows = lax.dynamic_slice_in_dim(column_one, second_panel * PB, PB, 0)
    updated = core_block[:, PB:] - jnp.dot(column_one, cross_rows.T, precision=HIGHEST)
    diag_two = lax.dynamic_slice_in_dim(updated, second_panel * PB, PB, 0)
    lower_two = jnp.linalg.cholesky(diag_two)
    inverse_two = jax.scipy.linalg.solve_triangular(lower_two, identity, lower=True)
    column_two = jnp.dot(updated, inverse_two.T, precision=HIGHEST)
    factor = jnp.concatenate([column_one, column_two], 1)
    return (factor, inverse_one, inverse_two, cross_rows)


def solve_basis(panel_one, panel_two, inverse_one, inverse_two, cross_rows):
    basis_one = jnp.dot(
        panel_one, inverse_one.T.astype(BF16), preferred_element_type=F32
    ).astype(BF16)
    partial_two = (
        panel_two.astype(F32)
        - jnp.dot(basis_one, cross_rows.T.astype(BF16), preferred_element_type=F32)
    ).astype(BF16)
    basis_two = jnp.dot(
        partial_two, inverse_two.T.astype(BF16), preferred_element_type=F32
    ).astype(BF16)
    return jnp.concatenate([basis_one, basis_two], 1)


def any_groups(sketch, stiffness, reaction, panel_order):
    cell_count, local_width = sketch.shape
    padded = with_halo(sketch, (("rows", 0),), NY)
    zfield = apply_operator(padded, cell_count, sketch, stiffness, reaction)
    groups = lax.axis_size("cols")
    own_group = lax.axis_index("cols")
    cell_total = cell_count * lax.axis_size("rows")
    first_panel = panel_order[0]
    second_panel = panel_order[1]
    slice_rows = cell_count // groups
    panels_here = local_width // PB

    def own_panel(panel_index):
        return lax.dynamic_slice_in_dim(zfield, panel_index % panels_here * PB, PB, 1)

    panel_one = spread(own_panel(first_panel), "cols", first_panel // panels_here)
    panel_two = spread(own_panel(second_panel), "cols", second_panel // panels_here)
    panels_both = jnp.concatenate([panel_one, panel_two], 1)
    partial_value = lax.dot_general(zfield, panels_both, CELLS_FIRST, preferred_element_type=F32)
    summed = lax.psum(partial_value, "rows")
    gram_full = lax.all_gather(summed, "cols", axis=0, tiled=True)
    factor, inverse_one, inverse_two, cross_rows = factorize(
        gram_full, first_panel, second_panel, cell_total
    )
    basis_full = solve_basis(panel_one, panel_two, inverse_one, inverse_two, cross_rows)
    own_factor = lax.dynamic_slice_in_dim(factor, own_group * local_width, local_width, 0).astype(
        BF16
    )
    residual = (
        zfield.astype(F32) - jnp.dot(basis_full, own_factor.T, preferred_element_type=F32)
    ).astype(BF16)
    basis_rows = lax.dynamic_slice_in_dim(basis_full, own_group * slice_rows, slice_rows, 0)
    factor_cols = lax.dynamic_slice_in_dim(factor, own_group * local_width, local_width, 0)
    return (residual, basis_rows, factor_cols)


def column_of(row):
    return jnp.transpose(jnp.broadcast_to(row, (LANES, LANES)))


WIDE = LANES + 32
PIECES = NY // LANES


def beside(lead):
    row = lax.broadcasted_iota(jnp.int32, (LANES, WIDE), 0) + lead
    col = lax.broadcasted_iota(jnp.int32, (LANES, WIDE), 1)
    return jnp.where((col == row - 1) | (col == row + 1), 1.0, 0.0).astype(BF16)


def neighbours():
    return {lead: beside(lead) for lead in (0, 16, 32)}


def stencil_piece(number, near, load, above, below, mix_col, stiff_col):
    lead = 0 if number == 0 else 32 if number == PIECES - 1 else 16
    wide = load(number * LANES - lead, WIDE)
    sides = jnp.dot(near[lead], wide, preferred_element_type=F32)
    around = (above.astype(F32) + below.astype(F32)) + sides
    centre = load(number * LANES, LANES).astype(F32)
    return (mix_col * centre - stiff_col * around).astype(BF16)


def panel_lines(sketch, mix, stiff, info, jobs, line_of, tile_of, low=None, high=None):
    last_line = sketch.shape[0] // NY - 1

    def body(info_ref, up_ref, mid_ref, down_ref, mix_ref, stiff_ref, *rest):
        out_ref = rest[-1]

        near = neighbours()

        def run(above, below):
            for number in range(PIECES):
                at = slice(number * LANES, (number + 1) * LANES)
                out_ref[at, :] = stencil_piece(
                    number,
                    near,
                    lambda start, size: mid_ref[start : start + size, :],
                    above[at, :],
                    below[at, :],
                    column_of(mix_ref[number : number + 1, :]),
                    column_of(stiff_ref[number : number + 1, :]),
                )

        if low is None:
            run(up_ref, down_ref)
        else:
            line = line_of(pl.program_id(0), info_ref)

            @pl.when(line == 0)
            def _():
                run(rest[0], down_ref)

            @pl.when(line == last_line)
            def _():
                run(up_ref, rest[1])

    def block(shift):
        return pl.BlockSpec(
            (NY, LANES),
            lambda j, t: (jnp.clip(line_of(j, t) + shift, 0, last_line), tile_of(j, t)),
        )

    coef = pl.BlockSpec((PIECES, LANES), lambda j, t: (line_of(j, t), 0))
    halo = pl.BlockSpec((NY, LANES), lambda j, t: (0, 0))
    extra = [] if low is None else [low, high]
    return pl.pallas_call(
        body,
        grid_spec=pltpu.PrefetchScalarGridSpec(
            num_scalar_prefetch=1,
            grid=(jobs,),
            in_specs=[block(-1), block(0), block(1), coef, coef] + [halo] * len(extra),
            out_specs=pl.BlockSpec((NY, LANES), lambda j, t: (0, j)),
        ),
        out_shape=jax.ShapeDtypeStruct((NY, jobs * LANES), BF16),
        compiler_params=pltpu.CompilerParams(vmem_limit_bytes=VMEM_BYTES),
        cost_estimate=LITTLE,
        name="panel_lines",
    )(info, sketch, sketch, sketch, mix, stiff, *extra)


def field_part(sketch, mix, stiff, info, panels, jobs, stride, line_of, sources, base=None):
    cells, width = sketch.shape
    arrays = []
    for copies in sources:
        for array, *_ in copies:
            if not any(array is known for known in arrays):
                arrays.append(array)
    index = lambda array: [array is known for known in arrays].index(True)
    plan = [
        (slot, index(array), row, column, size, place)
        for slot, copies in enumerate(sources)
        for array, row, column, size, place in copies
    ]

    def body(info_ref, *refs):
        hbm, rest = refs[: len(arrays)], refs[len(arrays) :]
        mix_ref, stiff_ref = rest[:2]
        z_ref, gram_ref, lines_ref, acc_ref, sems = rest[-5:]
        step = pl.program_id(0)

        def copy_of(number):
            slot, which, row, column, size, place = plan[number]
            at = place(info_ref)
            at = at if isinstance(at, int) else pl.multiple_of(at, LANES)
            return pltpu.make_async_copy(
                hbm[which].at[row : row + NY, column : column + size],
                lines_ref.at[slot, :, pl.ds(at, size)],
                sems.at[number],
            )

        def wait_for(slots):
            for number, entry in enumerate(plan):
                if entry[0] in slots:
                    copy_of(number).wait()

        @pl.when(step == 0)
        def _():
            for number in range(len(plan)):
                copy_of(number).start()
            wait_for((0, 1, 2))

        for job in range(1, jobs):

            @pl.when(step == job)
            def _():
                wait_for([stride * job + k for k in range(3) if k >= 3 - stride])

        first = step * stride
        near = neighbours()
        for number in range(PIECES):
            at = slice(number * LANES, (number + 1) * LANES)
            mix_col = column_of(mix_ref[number : number + 1, :])
            stiff_col = column_of(stiff_ref[number : number + 1, :])
            for tile in range(width // LANES):
                cols = slice(tile * LANES, (tile + 1) * LANES)
                z_ref[at, cols] = stencil_piece(
                    number,
                    near,
                    lambda start, size: lines_ref[first + 1, start : start + size, cols],
                    lines_ref[first, at, cols],
                    lines_ref[first + 2, at, cols],
                    mix_col,
                    stiff_col,
                )

        own = [
            z_ref[:, pl.ds(pl.multiple_of(info_ref[1 + k] * PB, PB), PB)] for k in range(panels)
        ]
        own = own[0] if panels == 1 else jnp.concatenate(own, 1)
        product = lax.dot_general(own, z_ref[...], CELLS_FIRST, preferred_element_type=F32)

        @pl.when(step == 0)
        def _():
            acc_ref[...] = product

        @pl.when(step > 0)
        def _():
            acc_ref[...] += product

        @pl.when(step == jobs - 1)
        def _():
            gram_ref[...] = jnp.transpose(acc_ref[...])

    coef = pl.BlockSpec((PIECES, LANES), lambda j, t: (line_of(j, t), 0))
    ANY = pl.BlockSpec(memory_space=pl.ANY)
    extra = [] if base is None else [base]
    return pl.pallas_call(
        body,
        grid_spec=pltpu.PrefetchScalarGridSpec(
            num_scalar_prefetch=1,
            grid=(jobs,),
            in_specs=[ANY] * len(arrays) + [coef, coef] + [ANY] * len(extra),
            out_specs=[
                pl.BlockSpec((NY, width), lambda j, t: (line_of(j, t), 0)),
                pl.BlockSpec((width, panels * PB), lambda j, t: (0, 0)),
            ],
            scratch_shapes=[
                pltpu.VMEM((len(sources), NY, width), BF16),
                pltpu.VMEM((panels * PB, width), F32),
                pltpu.SemaphoreType.DMA((len(plan),)),
            ],
        ),
        out_shape=[
            jax.ShapeDtypeStruct((cells, width), BF16),
            jax.ShapeDtypeStruct((width, panels * PB), F32),
        ],
        input_output_aliases={} if base is None else {3 + len(arrays): 0},
        compiler_params=pltpu.CompilerParams(vmem_limit_bytes=VMEM_BYTES),
        cost_estimate=LITTLE,
        name="field_part",
    )(info, *arrays, mix, stiff, *extra)


def whole_field(sketch, mix, stiff, info, panels, low, high):
    width = sketch.shape[1]
    lines = sketch.shape[0] // NY

    def line(number):
        return [(sketch, number * NY, 0, width, lambda t: 0)]

    field, gram = field_part(
        sketch,
        mix,
        stiff,
        info,
        panels,
        lines - 2,
        1,
        lambda j, t: j + 1,
        [line(k) for k in range(lines)],
    )
    field, more = field_part(
        sketch,
        mix,
        stiff,
        info,
        panels,
        2,
        3,
        lambda j, t: j * (lines - 1),
        [low, line(0), line(1), line(lines - 2), line(lines - 1), high],
        field,
    )
    return field, gram + more


def copy_lines(source, info, jobs, line_of, tile_of, width=LANES):
    def body(info_ref, z_ref, out_ref):
        out_ref[...] = z_ref[...]

    return pl.pallas_call(
        body,
        grid_spec=pltpu.PrefetchScalarGridSpec(
            num_scalar_prefetch=1,
            grid=(jobs,),
            in_specs=[pl.BlockSpec((NY, width), lambda j, t: (line_of(j, t), tile_of(j, t)))],
            out_specs=pl.BlockSpec((NY, width), lambda j, t: (0, j)),
        ),
        out_shape=jax.ShapeDtypeStruct((NY, jobs * width), BF16),
        compiler_params=pltpu.CompilerParams(vmem_limit_bytes=VMEM_BYTES),
        cost_estimate=LITTLE,
        name="copy_lines",
    )(info, source)


def take_halos(sketch, info, own_tile, tile_after):
    cells, width = sketch.shape
    jobs = width // LANES
    last = cells // NY - 1

    def body(info_ref, bottom_ref, top_ref, low_own, high_own, low_rest, high_rest):
        first = pl.program_id(0) == 0

        @pl.when(first)
        def _():
            low_own[...] = bottom_ref[...]
            high_own[...] = top_ref[...]

        @pl.when(jnp.logical_not(first))
        def _():
            low_rest[...] = bottom_ref[...]
            high_rest[...] = top_ref[...]

    def tile(j, t):
        return jnp.where(j == 0, own_tile(j, t), tile_after(j - 1, t))

    one = pl.BlockSpec((NY, LANES), lambda j, t: (0, 0))
    rest = pl.BlockSpec((NY, LANES), lambda j, t: (0, jnp.maximum(j - 1, 0)))
    return pl.pallas_call(
        body,
        grid_spec=pltpu.PrefetchScalarGridSpec(
            num_scalar_prefetch=1,
            grid=(jobs,),
            in_specs=[
                pl.BlockSpec((NY, LANES), lambda j, t: (last, tile(j, t))),
                pl.BlockSpec((NY, LANES), lambda j, t: (0, tile(j, t))),
            ],
            out_specs=[one, one, rest, rest],
        ),
        out_shape=[jax.ShapeDtypeStruct((NY, LANES), BF16)] * 2
        + [jax.ShapeDtypeStruct((NY, (jobs - 1) * LANES), BF16)] * 2,
        compiler_params=pltpu.CompilerParams(vmem_limit_bytes=VMEM_BYTES),
        cost_estimate=LITTLE,
        name="take_halos",
    )(info, sketch, sketch)


def gram_parts(zfield, parts, info, line_of):
    width = zfield.shape[1]
    starts = [sum(count for _, count in parts[:k]) for k in range(len(parts))]
    jobs = sum(count for _, count in parts)

    def body(info_ref, z_ref, *rest):
        out_ref, acc_ref = rest[-2:]
        step = pl.program_id(0)

        @pl.when(step == 0)
        def _():
            acc_ref[...] = jnp.zeros_like(acc_ref)

        for ref, start, (_, count) in zip(rest, starts, parts):

            @pl.when((step >= start) & (step < start + count))
            def _(ref=ref):
                acc_ref[...] += lax.dot_general(
                    ref[...], z_ref[...], CELLS_FIRST, preferred_element_type=F32
                )

        @pl.when(step == jobs - 1)
        def _():
            out_ref[...] = jnp.transpose(acc_ref[...])

    def block(start, count):
        return pl.BlockSpec((NY, PB), lambda j, t: (0, jnp.clip(j - start, 0, count - 1)))

    return pl.pallas_call(
        body,
        grid_spec=pltpu.PrefetchScalarGridSpec(
            num_scalar_prefetch=1,
            grid=(jobs,),
            in_specs=[pl.BlockSpec((NY, width), lambda j, t: (line_of(j, t), 0))]
            + [block(start, count) for start, (_, count) in zip(starts, parts)],
            out_specs=pl.BlockSpec((width, PB), lambda j, t: (0, 0)),
            scratch_shapes=[pltpu.VMEM((PB, width), F32)],
        ),
        out_shape=jax.ShapeDtypeStruct((width, PB), F32),
        compiler_params=pltpu.CompilerParams(vmem_limit_bytes=VMEM_BYTES),
        cost_estimate=LITTLE,
        name="gram_parts",
    )(info, zfield, *[array for array, _ in parts])


def gram_lines(zfield, others, info, jobs, line_of):
    width = zfield.shape[1]
    total = sum(columns for _, columns, _ in others)

    def body(info_ref, z_ref, *rest):
        out_ref, acc_ref = rest[-2:]
        step = pl.program_id(0)
        parts = [ref[...] for ref in rest[:-2]]
        right = parts[0] if len(parts) == 1 else jnp.concatenate(parts, 1)
        product = lax.dot_general(right, z_ref[...], CELLS_FIRST, preferred_element_type=F32)

        @pl.when(step == 0)
        def _():
            acc_ref[...] = product

        @pl.when(step > 0)
        def _():
            acc_ref[...] += product

        @pl.when(step == jobs - 1)
        def _():
            out_ref[...] = jnp.transpose(acc_ref[...])

    return pl.pallas_call(
        body,
        grid_spec=pltpu.PrefetchScalarGridSpec(
            num_scalar_prefetch=1,
            grid=(jobs,),
            in_specs=[pl.BlockSpec((NY, width), lambda j, t: (line_of(j, t), 0))]
            + [pl.BlockSpec((NY, columns), block) for _, columns, block in others],
            out_specs=pl.BlockSpec((width, total), lambda j, t: (0, 0)),
            scratch_shapes=[pltpu.VMEM((total, width), F32)],
        ),
        out_shape=jax.ShapeDtypeStruct((width, total), F32),
        compiler_params=pltpu.CompilerParams(vmem_limit_bytes=VMEM_BYTES),
        cost_estimate=LITTLE,
        name="gram_lines",
    )(info, zfield, *[array for array, _, _ in others])


def inverse_factor(block):
    def body(a_ref, o_ref, work):
        sub = lax.broadcasted_iota(jnp.int32, (8, PB), 0)
        row = lax.broadcasted_iota(jnp.int32, (PB, PB), 0)
        lane = lax.broadcasted_iota(jnp.int32, (PB, PB), 1)
        work[:, :PB] = a_ref[...]
        work[:, PB:] = (row == lane).astype(F32)

        def spread_row(value, s):
            return jnp.broadcast_to(value[s : s + 1, :], (8, PB))

        @pl.loop(0, PB // 8)
        def _(step):
            at = pl.ds(pl.multiple_of(step * 8, 8), 8)
            left, right = work[at, :PB], work[at, PB:]
            near = pltpu.roll(left, (PB - step * 8) % PB, 1)
            columns = [jnp.broadcast_to(near[:, c : c + 1], (8, PB)) for c in range(8)]
            for s in range(8):
                scale = lax.rsqrt(spread_row(columns[s], s))
                row_left = spread_row(left, s) * scale
                row_right = spread_row(right, s) * scale
                weight = jnp.where(sub > s, columns[s] * scale, 0.0)
                left = jnp.where(sub == s, row_left, left - weight * row_left)
                right = jnp.where(sub == s, row_right, right - weight * row_right)
                for c in range(s + 1, 8):
                    columns[c] = columns[c] - weight * (spread_row(columns[s], c) * scale)
            o_ref[at, :] = right
            both = jnp.concatenate([left, right], 1)
            work[...] -= lax.dot_general(
                left, both, CELLS_FIRST, precision=HIGHEST, preferred_element_type=F32
            )

    return pl.pallas_call(
        body,
        out_shape=jax.ShapeDtypeStruct((PB, PB), F32),
        scratch_shapes=[pltpu.VMEM((PB, 2 * PB), F32)],
        cost_estimate=pl.CostEstimate(
            flops=8 << 30, bytes_accessed=PB * PB * 8, transcendentals=PB
        ),
        name="inverse_factor",
    )(block)


def finish(zfield, chunks, solves, factor, info, pair, slot_of):
    cells, width = zfield.shape
    lines = cells // NY
    block = 2 * PB if pair else PB
    arrays = []
    for array, _ in chunks:
        if not any(array is known for known in arrays):
            arrays.append(array)
    index = lambda array: [array is known for known in arrays].index(True)

    def body(t, *refs):
        hbm, rest = refs[: len(arrays)], refs[len(arrays) :]
        z_ref, one_ref, cross_ref, two_ref, f_ref, out_ref, half_ref = rest[:7]
        got_ref, pan_ref, bas_ref, sems = rest[7:]
        step = pl.program_id(0)
        role = t[0]

        def copy_of(slot):
            array, column = chunks[slot]
            return pltpu.make_async_copy(
                hbm[index(array)].at[:, column : column + block], got_ref.at[slot], sems.at[slot]
            )

        @pl.when(step == 0)
        def _():
            for slot in range(lines):
                copy_of(slot).start()

        mine = slot_of(step, t)
        for slot in range(lines):

            @pl.when(mine == slot)
            def _():
                copy_of(slot).wait()

        def tile(which):
            return z_ref[:, pl.ds(pl.multiple_of(t[which] * PB, PB), PB)]

        @pl.when(role == 0)
        def _():
            pan_ref[:, :PB] = tile(1)
            pan_ref[:, PB:] = tile(2) if pair else got_ref[mine]

        @pl.when(role != 0)
        def _():
            if pair:
                pan_ref[...] = got_ref[mine]
            else:
                pan_ref[:, :PB] = got_ref[mine]
                pan_ref[:, PB:] = tile(1)

        one = lax.dot_general(
            pan_ref[:, :PB], one_ref[...], LAST_LAST, preferred_element_type=F32
        ).astype(BF16)
        partial = (
            pan_ref[:, PB:].astype(F32)
            - lax.dot_general(one, cross_ref[...], LAST_LAST, preferred_element_type=F32)
        ).astype(BF16)
        two = lax.dot_general(
            partial, two_ref[...], LAST_LAST, preferred_element_type=F32
        ).astype(BF16)
        bas_ref[:, :PB] = one
        bas_ref[:, PB:] = two
        out_ref[...] = (
            z_ref[...].astype(F32)
            - lax.dot_general(
                bas_ref[...], f_ref[...], LAST_LAST, preferred_element_type=F32
            )
        ).astype(BF16)

        @pl.when(step // (lines // 2) == t[3])
        def _():
            half_ref[...] = bas_ref[...]

    small = pl.BlockSpec((PB, PB), lambda j, t: (0, 0))
    line = pl.BlockSpec((NY, width), lambda j, t: (j, 0))
    last = lines // 2 - 1
    return pl.pallas_call(
        body,
        grid_spec=pltpu.PrefetchScalarGridSpec(
            num_scalar_prefetch=1,
            grid=(lines,),
            in_specs=[pl.BlockSpec(memory_space=pl.ANY)] * len(arrays)
            + [line, small, small, small, pl.BlockSpec((width, 2 * PB), lambda j, t: (0, 0))],
            out_specs=[
                line,
                pl.BlockSpec(
                    (NY, 2 * PB), lambda j, t: (jnp.clip(j - t[3] * (last + 1), 0, last), 0)
                ),
            ],
            scratch_shapes=[
                pltpu.VMEM((lines, NY, block), BF16),
                pltpu.VMEM((NY, 2 * PB), BF16),
                pltpu.VMEM((NY, 2 * PB), BF16),
                pltpu.SemaphoreType.DMA((lines,)),
            ],
        ),
        out_shape=[
            jax.ShapeDtypeStruct((cells, width), BF16),
            jax.ShapeDtypeStruct((cells // 2, 2 * PB), BF16),
        ],
        compiler_params=pltpu.CompilerParams(vmem_limit_bytes=VMEM_BYTES),
        cost_estimate=LITTLE,
        name="finish",
    )(info, *arrays, zfield, *solves, factor)


def swap(value):
    return lax.ppermute(value, "cols", SWAP)


def bit_of(bit):
    return lax.axis_index("rows") // bit % 2


def row_bits():
    count = lax.axis_size("rows")
    return [1 << k for k in range(count.bit_length() - 1)]


def over_rows(value, bit):
    count = lax.axis_size("rows")
    return lax.ppermute(value, "rows", [(k, k ^ bit) for k in range(count)])


def sum_rows(value):
    for bit in row_bits():
        value = value + over_rows(value, bit)
    return value


def reduce_rows(split, whole=None):
    for bit in row_bits():
        half = split.shape[0] // 2
        side = bit_of(bit)
        keep = lax.dynamic_slice_in_dim(split, side * half, half, 0)
        send = lax.dynamic_slice_in_dim(split, (1 - side) * half, half, 0)
        if whole is None:
            split = keep + over_rows(send, bit)
        else:
            got = over_rows(jnp.concatenate([send, whole], 0), bit)
            split = keep + got[:half]
            whole = whole + got[half:]
    return split, whole


def slice_start(width):
    start = 0
    for bit in row_bits():
        width //= 2
        start = start + bit_of(bit) * width
    return start


def gather_rows(value):
    for bit in reversed(row_bits()):
        other = over_rows(value, bit)
        value = jnp.where(
            bit_of(bit) == 0,
            jnp.concatenate([value, other], 0),
            jnp.concatenate([other, value], 0),
        )
    return value


def dot_t(left, right):
    return lax.dot_general(left, right, LAST_LAST, precision=HIGHEST, preferred_element_type=F32)


def step_of(live, work, *values):
    shapes = jax.eval_shape(work, *values)
    empty = lambda *_: jax.tree.map(lambda shape: jnp.zeros(shape.shape, shape.dtype), shapes)
    return lax.cond(live, work, empty, *values)


def after(value, *events):
    return lax.optimization_barrier((value, *events))[0]


def two_groups(sketch, stiffness, reaction, panel_order):
    cells, width = sketch.shape
    lines = cells // NY
    panels_here = width // PB
    row_count = lax.axis_size("rows")
    scale = 1.0 / (cells * row_count)
    group = lax.axis_index("cols")
    first, second = panel_order[0], panel_order[1]
    group_one, group_two = first // panels_here, second // panels_here
    share = width // row_count
    eye = jnp.eye(PB, dtype=F32)
    tile_one = first % panels_here
    tile_two = second % panels_here
    holds_one = group == group_one
    role = jnp.where(holds_one, 0, 1)

    def upward(value):
        return lax.ppermute(value, "rows", [(i, i + 1) for i in range(row_count - 1)])

    def downward(value):
        return lax.ppermute(value, "rows", [(i + 1, i) for i in range(row_count - 1)])

    def identity_rows(panel):
        position = group * width + slice_start(width) + jnp.arange(share, dtype=jnp.int32)
        offset = jnp.arange(PB, dtype=jnp.int32)
        return (position[:, None] == panel * PB + offset[None, :]).astype(F32)

    def factor_of(one, two, inverse_one, cross, inverse_two):
        core_one = one * scale + identity_rows(first)
        core_two = two * scale + identity_rows(second)
        column_one = dot_t(core_one, inverse_one)
        column_two = dot_t(core_two - dot_t(column_one, cross), inverse_two)
        return gather_rows(jnp.concatenate([column_one, column_two], 1))

    def apart(sketch, mix, stiff, info):
        def order(slot, turned):
            turned = jnp.asarray(turned, jnp.int32)
            near = (slot + 1) & 3
            return jnp.where((slot < 4) == (turned == 0), near, (slot & 3) + 4)

        def sent(slot):
            return lambda j, t: order(slot + j, t[0])

        def came(slot):
            return lambda j, t: order(slot + j, 1 - t[0])

        own_tile = lambda j, t: t[1]
        tile_after = lambda j, t: (t[1] + 1 + j) % panels_here
        bottom, top = lambda j, t: lines - 1, lambda j, t: 0
        early = panel_lines(sketch, mix, stiff, info, 3, sent(0), own_tile)
        got_early = swap(early)
        others = panels_here - 1

        def own_halo(sketch, info):
            low, high, low_rest, high_rest = take_halos(sketch, info, own_tile, tile_after)
            return upward(low), downward(high), low_rest, high_rest

        live = info[3] >= 0
        low_own, high_own, low_rest, high_rest = step_of(
            live, own_halo, after(sketch, early), info
        )
        edges = panel_lines(
            sketch,
            mix,
            stiff,
            info,
            2,
            lambda j, t: order(3 + 4 * j, t[0]),
            own_tile,
            low_own,
            high_own,
        )
        edge, last = edges[:, :PB], edges[:, PB:]
        late = panel_lines(after(sketch, edge), mix, stiff, info, 3, sent(4), own_tile)
        got_late = swap(late)
        got_edge = swap(edge)
        got_last = swap(after(last, late, edge))

        def halo_copies(own, rest):
            copies = [(own, 0, 0, PB, lambda t: t[1] * PB)]
            for j in range(others):
                copies.append((rest, 0, j * PB, PB, lambda t, j=j: tile_after(j, t) * PB))
            return copies

        def local_field(sketch, mix, stiff, info, low_own, high_own, low_rest, high_rest):
            low_rest, high_rest = upward(low_rest), downward(high_rest)
            low, high = halo_copies(low_own, low_rest), halo_copies(high_own, high_rest)
            return whole_field(sketch, mix, stiff, info, 1, low, high)

        zfield, own = step_of(
            live,
            local_field,
            after(sketch, late, edges),
            mix,
            stiff,
            info,
            low_own,
            high_own,
            low_rest,
            high_rest,
        )
        many = gram_parts(
            zfield,
            [(got_early, 3), (got_late, 3)],
            info,
            lambda j, t: order(jnp.where(j < 3, j, j + 1), 1 - t[0]),
        )
        few = gram_parts(
            zfield,
            [(after(got_edge, many), 1), (after(got_last, many), 1)],
            info,
            lambda j, t: order(3 + 4 * j, 1 - t[0]),
        )

        def all_sums(own, other, info):
            own_rows = lambda value: lax.dynamic_slice_in_dim(value, info[1] * PB, PB, 0)
            both = jnp.concatenate([own, other], 1)
            shares, whole = reduce_rows(both, own_rows(both))
            own_share, other_share = shares[:, :PB], shares[:, PB:]
            diag_own, mixed_own = whole[:, :PB], whole[:, PB:]
            inverse_own = inverse_factor(diag_own * scale + eye)
            got = swap(jnp.where(holds_one, inverse_own, diag_own))
            inverse_one = jnp.where(holds_one, inverse_own, got)
            diag_two = jnp.where(holds_one, got, diag_own)
            cross = dot_t(jnp.where(holds_one, mixed_own.T, mixed_own) * scale, inverse_one)
            inverse_two = inverse_factor(diag_two * scale + eye - dot_t(cross, cross))
            one = jnp.where(holds_one, own_share, other_share)
            two = jnp.where(holds_one, other_share, own_share)
            factor = factor_of(one, two, inverse_one, cross, inverse_two)
            return factor, inverse_one, cross, inverse_two

        factor, inverse_one, cross, inverse_two = step_of(live, all_sums, own, many + few, info)

        def slot_of(line, t):
            near = (line + 3) & 3
            return jnp.where(
                t[0] == 0, jnp.where(line < 4, near + 4, line - 4), jnp.where(line < 4, near, line)
            )

        solves = [value.astype(BF16) for value in (inverse_one, cross, inverse_two)]
        chunks = [(got_early, 0), (got_early, PB), (got_early, 2 * PB), (got_edge, 0)]
        chunks += [(got_late, 0), (got_late, PB), (got_late, 2 * PB), (got_last, 0)]
        residual, basis_rows = finish(
            zfield, chunks, solves, factor.astype(BF16), info, False, slot_of
        )
        return residual, basis_rows, factor

    def together(sketch, mix, stiff, info):
        owner = holds_one
        pairs = [(1, 2), (3, 4), (0, 7), (5, 6)]

        def tile_at(j, t):
            return jnp.where(j % 2 == 0, t[1], t[2])

        def chunk(near, far):
            return panel_lines(
                sketch,
                mix,
                stiff,
                info,
                4,
                lambda j, t: jnp.where(t[0] == 0, near + j // 2, far),
                lambda j, t: jnp.where(t[0] == 0, tile_at(j, t), j),
            )

        chunk_one = chunk(1, 5)
        got_one = swap(chunk_one)
        chunk_two = chunk(3, 6)
        got_two = swap(chunk_two)
        live = info[3] >= 0
        nothing = lambda j, t: 0
        whole_line = lambda halo: [(halo, 0, 0, width, lambda t: 0)]

        def local_field(sketch, mix, stiff, info):
            low = upward(copy_lines(sketch, info, 1, lambda j, t: lines - 1, nothing, width))
            high = downward(copy_lines(sketch, info, 1, nothing, nothing, width))
            zfield, own = whole_field(
                sketch, mix, stiff, info, 2, whole_line(low), whole_line(high)
            )
            return zfield, own, copy_lines(zfield, info, 4, lambda j, t: j // 2 * 7, tile_at)

        sketch = after(sketch, chunk_one, chunk_two)
        zfield, own, chunk_three = step_of(live, local_field, sketch, mix, stiff, info)
        got_three = swap(chunk_three)

        def owner_part(zfield, received, line, info):
            return gram_lines(
                received,
                [
                    (zfield, PB, lambda j, t: (line, t[1])),
                    (zfield, PB, lambda j, t: (line, t[2])),
                ],
                info,
                1,
                lambda j, t: 0,
            )

        def other_part(zfield, received, pair, info):
            return gram_lines(
                zfield,
                [(received, 2 * PB, lambda j, t: (0, j))],
                info,
                2,
                lambda j, t: pair[0] + j * (pair[1] - pair[0]),
            )

        def own_sums(own, owner_sum, info):
            shares, _ = reduce_rows(jnp.concatenate([own, owner_sum], 1))
            own_share, owner_share = shares[:, : 2 * PB], shares[:, 2 * PB :]
            total = gather_rows(own_share)
            return own_share, owner_share, *[
                lax.dynamic_slice_in_dim(total, info[k] * PB, PB, 0) for k in (1, 2)
            ]

        own = after(own, chunk_three)
        owner_sum = owner_part(zfield, got_one, 5, info)
        other_sum = other_part(zfield, got_one, pairs[0], info)
        late_two = after(got_two, owner_sum, other_sum)
        owner_sum = owner_sum + owner_part(zfield, late_two, 6, info)
        own_share, owner_share, diag_one, diag_two = step_of(live, own_sums, own, owner_sum, info)
        small = jnp.concatenate([diag_one, diag_two, owner_share], 0)
        got_small = swap(small)
        chunk_four = copy_lines(zfield, info, 4, lambda j, t: 5 + j // 2, tile_at)
        got_four = swap(after(chunk_four, got_small))
        other_sum = other_sum + other_part(zfield, after(late_two, small), pairs[1], info)
        other_sum = other_sum + other_part(zfield, after(got_three, small), pairs[2], info)
        diag = jnp.where(owner, small[: 2 * PB], got_small[: 2 * PB])
        extra = got_small[2 * PB :]

        def last_sums(other_sum, own_share, extra, diag):
            inverse_one = inverse_factor(diag[:PB, :PB] * scale + eye)
            cross = dot_t(diag[PB:, :PB] * scale, inverse_one)
            inverse_two = inverse_factor(diag[PB:, PB:] * scale + eye - dot_t(cross, cross))
            other_share, _ = reduce_rows(other_sum)
            mine = jnp.where(owner, own_share, other_share + extra)
            factor = factor_of(mine[:, :PB], mine[:, PB:], inverse_one, cross, inverse_two)
            return factor, inverse_one, cross, inverse_two

        factor, inverse_one, cross, inverse_two = step_of(
            live, last_sums, after(other_sum, chunk_four), own_share, extra, diag
        )

        def slot_of(line, t):
            return jnp.where(line == 0, 4, jnp.where(line == 7, 5, jnp.where(line < 5, line - 1, line + 1)))

        solves = [value.astype(BF16) for value in (inverse_one, cross, inverse_two)]
        chunks = [
            (array, column)
            for array in (got_one, got_two, got_three, after(got_four, factor))
            for column in (0, 2 * PB)
        ]
        residual, basis_rows = finish(
            zfield, chunks, solves, factor.astype(BF16), info, True, slot_of
        )
        return residual, basis_rows, factor

    stiff = stiffness.reshape(-1, LANES)
    mix = (reaction + 4.0 * stiffness).reshape(-1, LANES)
    same = group_one == group_two
    info = jnp.stack(
        [
            role,
            jnp.where(same | holds_one, tile_one, tile_two),
            jnp.where(same | (role == 1), tile_two, tile_one),
            group,
        ]
    ).astype(jnp.int32)
    return lax.cond(same, together, apart, sketch, mix, stiff, info)


def per_device(sketch, stiffness, reaction, panel_order):
    cells, width = sketch.shape
    rows = lax.axis_size("rows")
    fits = lax.axis_size("cols") == 2 and cells == 8 * NY and width == 4 * PB
    if fits and rows & (rows - 1) == 0 and rows > 1:
        return two_groups(sketch, stiffness, reaction, panel_order)
    return any_groups(sketch, stiffness, reaction, panel_order)


def solution(mesh):
    return jax.shard_map(
        per_device,
        mesh=mesh,
        in_specs=(P("rows", "cols"), P("rows"), P("rows"), P()),
        out_specs=(P("rows", "cols"), P(("rows", "cols"), None), P("cols", None)),
        check_vma=False,
    )
```

```python
import jax
import jax.numpy as jnp
from jax import lax
from jax.experimental import pallas as pl
from jax.experimental.pallas import tpu as pltpu
from jax.sharding import PartitionSpec as P

PB = 128
NY = 2048
LANES = 128
BF16 = jnp.bfloat16
F32 = jnp.float32
HIGHEST = lax.Precision.HIGHEST
SWAP = [(0, 1), (1, 0)]
VMEM_BYTES = 56 << 20
LITTLE = pl.CostEstimate(flops=1 << 20, bytes_accessed=1 << 14, transcendentals=0)
CELLS_FIRST = (((0,), (0,)), ((), ()))
LAST_LAST = (((1,), (1,)), ((), ()))


def with_halo(block, sides, width):
    for axis, dim in sides:
        count = lax.axis_size(axis)
        forward = [(i, i + 1) for i in range(count - 1)]
        backward = [(target, source) for source, target in forward]
        low = lax.ppermute(
            lax.slice_in_dim(block, block.shape[dim] - width, None, axis=dim), axis, forward
        )
        high = lax.ppermute(lax.slice_in_dim(block, 0, width, axis=dim), axis, backward)
        block = jnp.concatenate([low, block, high], axis=dim)
    return block


def spread(value, axis, source):
    kept = jnp.where(lax.axis_index(axis) == source, value, 0).astype(value.dtype)
    return lax.psum(kept, axis)


def apply_operator(padded, cell_count, sketch, stiffness, reaction):
    centre = sketch.astype(jnp.float32)
    along_y = jnp.arange(cell_count) % NY
    upward = padded[:cell_count].astype(jnp.float32)
    downward = padded[2 * NY : 2 * NY + cell_count].astype(jnp.float32)
    leftward = jnp.where(
        (along_y == 0)[:, None], 0.0, padded[NY - 1 : NY - 1 + cell_count].astype(jnp.float32)
    )
    rightward = jnp.where(
        (along_y == NY - 1)[:, None], 0.0, padded[NY + 1 : NY + 1 + cell_count].astype(jnp.float32)
    )
    mixing = 4.0 * centre - upward - downward - leftward - rightward
    return (reaction[:, None] * centre + stiffness[:, None] * mixing).astype(jnp.bfloat16)


def factorize(gram_full, first_panel, second_panel, cell_total):
    width_all = gram_full.shape[0]
    positions = jnp.arange(width_all, dtype=jnp.int32)[:, None]
    offsets = jnp.arange(PB, dtype=jnp.int32)[None, :]
    ident_one = (positions == first_panel * PB + offsets).astype(jnp.float32)
    ident_two = (positions == second_panel * PB + offsets).astype(jnp.float32)
    core_block = gram_full / cell_total + jnp.concatenate([ident_one, ident_two], 1)
    diag_one = lax.dynamic_slice_in_dim(core_block[:, :PB], first_panel * PB, PB, 0)
    lower_one = jnp.linalg.cholesky(diag_one)
    identity = jnp.eye(PB, dtype=lower_one.dtype)
    inverse_one = jax.scipy.linalg.solve_triangular(lower_one, identity, lower=True)
    column_one = jnp.dot(core_block[:, :PB], inverse_one.T, precision=HIGHEST)
    cross_rows = lax.dynamic_slice_in_dim(column_one, second_panel * PB, PB, 0)
    updated = core_block[:, PB:] - jnp.dot(column_one, cross_rows.T, precision=HIGHEST)
    diag_two = lax.dynamic_slice_in_dim(updated, second_panel * PB, PB, 0)
    lower_two = jnp.linalg.cholesky(diag_two)
    inverse_two = jax.scipy.linalg.solve_triangular(lower_two, identity, lower=True)
    column_two = jnp.dot(updated, inverse_two.T, precision=HIGHEST)
    factor = jnp.concatenate([column_one, column_two], 1)
    return (factor, inverse_one, inverse_two, cross_rows)


def solve_basis(panel_one, panel_two, inverse_one, inverse_two, cross_rows):
    basis_one = jnp.dot(
        panel_one, inverse_one.T.astype(BF16), preferred_element_type=F32
    ).astype(BF16)
    partial_two = (
        panel_two.astype(F32)
        - jnp.dot(basis_one, cross_rows.T.astype(BF16), preferred_element_type=F32)
    ).astype(BF16)
    basis_two = jnp.dot(
        partial_two, inverse_two.T.astype(BF16), preferred_element_type=F32
    ).astype(BF16)
    return jnp.concatenate([basis_one, basis_two], 1)


def any_groups(sketch, stiffness, reaction, panel_order):
    cell_count, local_width = sketch.shape
    padded = with_halo(sketch, (("rows", 0),), NY)
    zfield = apply_operator(padded, cell_count, sketch, stiffness, reaction)
    groups = lax.axis_size("cols")
    own_group = lax.axis_index("cols")
    cell_total = cell_count * lax.axis_size("rows")
    first_panel = panel_order[0]
    second_panel = panel_order[1]
    slice_rows = cell_count // groups
    panels_here = local_width // PB

    def own_panel(panel_index):
        return lax.dynamic_slice_in_dim(zfield, panel_index % panels_here * PB, PB, 1)

    panel_one = spread(own_panel(first_panel), "cols", first_panel // panels_here)
    panel_two = spread(own_panel(second_panel), "cols", second_panel // panels_here)
    panels_both = jnp.concatenate([panel_one, panel_two], 1)
    partial_value = lax.dot_general(zfield, panels_both, CELLS_FIRST, preferred_element_type=F32)
    summed = lax.psum(partial_value, "rows")
    gram_full = lax.all_gather(summed, "cols", axis=0, tiled=True)
    factor, inverse_one, inverse_two, cross_rows = factorize(
        gram_full, first_panel, second_panel, cell_total
    )
    basis_full = solve_basis(panel_one, panel_two, inverse_one, inverse_two, cross_rows)
    own_factor = lax.dynamic_slice_in_dim(factor, own_group * local_width, local_width, 0).astype(
        BF16
    )
    residual = (
        zfield.astype(F32) - jnp.dot(basis_full, own_factor.T, preferred_element_type=F32)
    ).astype(BF16)
    basis_rows = lax.dynamic_slice_in_dim(basis_full, own_group * slice_rows, slice_rows, 0)
    factor_cols = lax.dynamic_slice_in_dim(factor, own_group * local_width, local_width, 0)
    return (residual, basis_rows, factor_cols)


def column_of(row):
    return jnp.transpose(jnp.broadcast_to(row, (LANES, LANES)))


WIDE = LANES + 32
PIECES = NY // LANES


def beside(lead):
    row = lax.broadcasted_iota(jnp.int32, (LANES, WIDE), 0) + lead
    col = lax.broadcasted_iota(jnp.int32, (LANES, WIDE), 1)
    return jnp.where((col == row - 1) | (col == row + 1), 1.0, 0.0).astype(BF16)


def neighbours():
    return {lead: beside(lead) for lead in (0, 16, 32)}


def stencil_piece(number, near, load, above, below, mix_col, stiff_col):
    lead = 0 if number == 0 else 32 if number == PIECES - 1 else 16
    wide = load(number * LANES - lead, WIDE)
    sides = jnp.dot(near[lead], wide, preferred_element_type=F32)
    around = (above.astype(F32) + below.astype(F32)) + sides
    centre = load(number * LANES, LANES).astype(F32)
    return (mix_col * centre - stiff_col * around).astype(BF16)


def panel_lines(sketch, mix, stiff, info, jobs, line_of, tile_of, low=None, high=None):
    last_line = sketch.shape[0] // NY - 1

    def body(info_ref, up_ref, mid_ref, down_ref, mix_ref, stiff_ref, *rest):
        out_ref = rest[-1]

        near = neighbours()

        def run(above, below):
            for number in range(PIECES):
                at = slice(number * LANES, (number + 1) * LANES)
                out_ref[at, :] = stencil_piece(
                    number,
                    near,
                    lambda start, size: mid_ref[start : start + size, :],
                    above[at, :],
                    below[at, :],
                    column_of(mix_ref[number : number + 1, :]),
                    column_of(stiff_ref[number : number + 1, :]),
                )

        if low is None:
            run(up_ref, down_ref)
        else:
            line = line_of(pl.program_id(0), info_ref)

            @pl.when(line == 0)
            def _():
                run(rest[0], down_ref)

            @pl.when(line == last_line)
            def _():
                run(up_ref, rest[1])

    def block(shift):
        return pl.BlockSpec(
            (NY, LANES),
            lambda j, t: (jnp.clip(line_of(j, t) + shift, 0, last_line), tile_of(j, t)),
        )

    coef = pl.BlockSpec((PIECES, LANES), lambda j, t: (line_of(j, t), 0))
    halo = pl.BlockSpec((NY, LANES), lambda j, t: (0, 0))
    extra = [] if low is None else [low, high]
    return pl.pallas_call(
        body,
        grid_spec=pltpu.PrefetchScalarGridSpec(
            num_scalar_prefetch=1,
            grid=(jobs,),
            in_specs=[block(-1), block(0), block(1), coef, coef] + [halo] * len(extra),
            out_specs=pl.BlockSpec((NY, LANES), lambda j, t: (0, j)),
        ),
        out_shape=jax.ShapeDtypeStruct((NY, jobs * LANES), BF16),
        compiler_params=pltpu.CompilerParams(vmem_limit_bytes=VMEM_BYTES),
        cost_estimate=LITTLE,
        name="panel_lines",
    )(info, sketch, sketch, sketch, mix, stiff, *extra)


def field_part(sketch, mix, stiff, info, panels, jobs, stride, line_of, sources, base=None):
    cells, width = sketch.shape
    arrays = []
    for copies in sources:
        for array, *_ in copies:
            if not any(array is known for known in arrays):
                arrays.append(array)
    index = lambda array: [array is known for known in arrays].index(True)
    plan = [
        (slot, index(array), row, column, size, place)
        for slot, copies in enumerate(sources)
        for array, row, column, size, place in copies
    ]

    def body(info_ref, *refs):
        hbm, rest = refs[: len(arrays)], refs[len(arrays) :]
        mix_ref, stiff_ref = rest[:2]
        z_ref, gram_ref, lines_ref, acc_ref, sems = rest[-5:]
        step = pl.program_id(0)

        def copy_of(number):
            slot, which, row, column, size, place = plan[number]
            at = place(info_ref)
            at = at if isinstance(at, int) else pl.multiple_of(at, LANES)
            return pltpu.make_async_copy(
                hbm[which].at[row : row + NY, column : column + size],
                lines_ref.at[slot, :, pl.ds(at, size)],
                sems.at[number],
            )

        def wait_for(slots):
            for number, entry in enumerate(plan):
                if entry[0] in slots:
                    copy_of(number).wait()

        @pl.when(step == 0)
        def _():
            for number in range(len(plan)):
                copy_of(number).start()
            wait_for((0, 1, 2))

        for job in range(1, jobs):

            @pl.when(step == job)
            def _():
                wait_for([stride * job + k for k in range(3) if k >= 3 - stride])

        first = step * stride
        near = neighbours()
        for number in range(PIECES):
            at = slice(number * LANES, (number + 1) * LANES)
            mix_col = column_of(mix_ref[number : number + 1, :])
            stiff_col = column_of(stiff_ref[number : number + 1, :])
            for tile in range(width // LANES):
                cols = slice(tile * LANES, (tile + 1) * LANES)
                z_ref[at, cols] = stencil_piece(
                    number,
                    near,
                    lambda start, size: lines_ref[first + 1, start : start + size, cols],
                    lines_ref[first, at, cols],
                    lines_ref[first + 2, at, cols],
                    mix_col,
                    stiff_col,
                )

        own = [
            z_ref[:, pl.ds(pl.multiple_of(info_ref[1 + k] * PB, PB), PB)] for k in range(panels)
        ]
        own = own[0] if panels == 1 else jnp.concatenate(own, 1)
        product = lax.dot_general(own, z_ref[...], CELLS_FIRST, preferred_element_type=F32)

        @pl.when(step == 0)
        def _():
            acc_ref[...] = product

        @pl.when(step > 0)
        def _():
            acc_ref[...] += product

        @pl.when(step == jobs - 1)
        def _():
            gram_ref[...] = jnp.transpose(acc_ref[...])

    coef = pl.BlockSpec((PIECES, LANES), lambda j, t: (line_of(j, t), 0))
    ANY = pl.BlockSpec(memory_space=pl.ANY)
    extra = [] if base is None else [base]
    return pl.pallas_call(
        body,
        grid_spec=pltpu.PrefetchScalarGridSpec(
            num_scalar_prefetch=1,
            grid=(jobs,),
            in_specs=[ANY] * len(arrays) + [coef, coef] + [ANY] * len(extra),
            out_specs=[
                pl.BlockSpec((NY, width), lambda j, t: (line_of(j, t), 0)),
                pl.BlockSpec((width, panels * PB), lambda j, t: (0, 0)),
            ],
            scratch_shapes=[
                pltpu.VMEM((len(sources), NY, width), BF16),
                pltpu.VMEM((panels * PB, width), F32),
                pltpu.SemaphoreType.DMA((len(plan),)),
            ],
        ),
        out_shape=[
            jax.ShapeDtypeStruct((cells, width), BF16),
            jax.ShapeDtypeStruct((width, panels * PB), F32),
        ],
        input_output_aliases={} if base is None else {3 + len(arrays): 0},
        compiler_params=pltpu.CompilerParams(vmem_limit_bytes=VMEM_BYTES),
        cost_estimate=LITTLE,
        name="field_part",
    )(info, *arrays, mix, stiff, *extra)


def whole_field(sketch, mix, stiff, info, panels, low, high):
    width = sketch.shape[1]
    lines = sketch.shape[0] // NY

    def line(number):
        return [(sketch, number * NY, 0, width, lambda t: 0)]

    field, gram = field_part(
        sketch,
        mix,
        stiff,
        info,
        panels,
        lines - 2,
        1,
        lambda j, t: j + 1,
        [line(k) for k in range(lines)],
    )
    field, more = field_part(
        sketch,
        mix,
        stiff,
        info,
        panels,
        2,
        3,
        lambda j, t: j * (lines - 1),
        [low, line(0), line(1), line(lines - 2), line(lines - 1), high],
        field,
    )
    return field, gram + more


def copy_lines(source, info, jobs, line_of, tile_of, width=LANES):
    def body(info_ref, z_ref, out_ref):
        out_ref[...] = z_ref[...]

    return pl.pallas_call(
        body,
        grid_spec=pltpu.PrefetchScalarGridSpec(
            num_scalar_prefetch=1,
            grid=(jobs,),
            in_specs=[pl.BlockSpec((NY, width), lambda j, t: (line_of(j, t), tile_of(j, t)))],
            out_specs=pl.BlockSpec((NY, width), lambda j, t: (0, j)),
        ),
        out_shape=jax.ShapeDtypeStruct((NY, jobs * width), BF16),
        compiler_params=pltpu.CompilerParams(vmem_limit_bytes=VMEM_BYTES),
        cost_estimate=LITTLE,
        name="copy_lines",
    )(info, source)


def take_halos(sketch, info, own_tile, tile_after):
    cells, width = sketch.shape
    jobs = width // LANES
    last = cells // NY - 1

    def body(info_ref, bottom_ref, top_ref, low_own, high_own, low_rest, high_rest):
        first = pl.program_id(0) == 0

        @pl.when(first)
        def _():
            low_own[...] = bottom_ref[...]
            high_own[...] = top_ref[...]

        @pl.when(jnp.logical_not(first))
        def _():
            low_rest[...] = bottom_ref[...]
            high_rest[...] = top_ref[...]

    def tile(j, t):
        return jnp.where(j == 0, own_tile(j, t), tile_after(j - 1, t))

    one = pl.BlockSpec((NY, LANES), lambda j, t: (0, 0))
    rest = pl.BlockSpec((NY, LANES), lambda j, t: (0, jnp.maximum(j - 1, 0)))
    return pl.pallas_call(
        body,
        grid_spec=pltpu.PrefetchScalarGridSpec(
            num_scalar_prefetch=1,
            grid=(jobs,),
            in_specs=[
                pl.BlockSpec((NY, LANES), lambda j, t: (last, tile(j, t))),
                pl.BlockSpec((NY, LANES), lambda j, t: (0, tile(j, t))),
            ],
            out_specs=[one, one, rest, rest],
        ),
        out_shape=[jax.ShapeDtypeStruct((NY, LANES), BF16)] * 2
        + [jax.ShapeDtypeStruct((NY, (jobs - 1) * LANES), BF16)] * 2,
        compiler_params=pltpu.CompilerParams(vmem_limit_bytes=VMEM_BYTES),
        cost_estimate=LITTLE,
        name="take_halos",
    )(info, sketch, sketch)


def gram_parts(zfield, parts, info, line_of):
    width = zfield.shape[1]
    starts = [sum(count for _, count in parts[:k]) for k in range(len(parts))]
    jobs = sum(count for _, count in parts)

    def body(info_ref, z_ref, *rest):
        out_ref, acc_ref = rest[-2:]
        step = pl.program_id(0)

        @pl.when(step == 0)
        def _():
            acc_ref[...] = jnp.zeros_like(acc_ref)

        for ref, start, (_, count) in zip(rest, starts, parts):

            @pl.when((step >= start) & (step < start + count))
            def _(ref=ref):
                acc_ref[...] += lax.dot_general(
                    ref[...], z_ref[...], CELLS_FIRST, preferred_element_type=F32
                )

        @pl.when(step == jobs - 1)
        def _():
            out_ref[...] = jnp.transpose(acc_ref[...])

    def block(start, count):
        return pl.BlockSpec((NY, PB), lambda j, t: (0, jnp.clip(j - start, 0, count - 1)))

    return pl.pallas_call(
        body,
        grid_spec=pltpu.PrefetchScalarGridSpec(
            num_scalar_prefetch=1,
            grid=(jobs,),
            in_specs=[pl.BlockSpec((NY, width), lambda j, t: (line_of(j, t), 0))]
            + [block(start, count) for start, (_, count) in zip(starts, parts)],
            out_specs=pl.BlockSpec((width, PB), lambda j, t: (0, 0)),
            scratch_shapes=[pltpu.VMEM((PB, width), F32)],
        ),
        out_shape=jax.ShapeDtypeStruct((width, PB), F32),
        compiler_params=pltpu.CompilerParams(vmem_limit_bytes=VMEM_BYTES),
        cost_estimate=LITTLE,
        name="gram_parts",
    )(info, zfield, *[array for array, _ in parts])


def gram_lines(zfield, others, info, jobs, line_of):
    width = zfield.shape[1]
    total = sum(columns for _, columns, _ in others)

    def body(info_ref, z_ref, *rest):
        out_ref, acc_ref = rest[-2:]
        step = pl.program_id(0)
        parts = [ref[...] for ref in rest[:-2]]
        right = parts[0] if len(parts) == 1 else jnp.concatenate(parts, 1)
        product = lax.dot_general(right, z_ref[...], CELLS_FIRST, preferred_element_type=F32)

        @pl.when(step == 0)
        def _():
            acc_ref[...] = product

        @pl.when(step > 0)
        def _():
            acc_ref[...] += product

        @pl.when(step == jobs - 1)
        def _():
            out_ref[...] = jnp.transpose(acc_ref[...])

    return pl.pallas_call(
        body,
        grid_spec=pltpu.PrefetchScalarGridSpec(
            num_scalar_prefetch=1,
            grid=(jobs,),
            in_specs=[pl.BlockSpec((NY, width), lambda j, t: (line_of(j, t), 0))]
            + [pl.BlockSpec((NY, columns), block) for _, columns, block in others],
            out_specs=pl.BlockSpec((width, total), lambda j, t: (0, 0)),
            scratch_shapes=[pltpu.VMEM((total, width), F32)],
        ),
        out_shape=jax.ShapeDtypeStruct((width, total), F32),
        compiler_params=pltpu.CompilerParams(vmem_limit_bytes=VMEM_BYTES),
        cost_estimate=LITTLE,
        name="gram_lines",
    )(info, zfield, *[array for array, _, _ in others])


def inverse_factor(block):
    def body(a_ref, o_ref, work):
        sub = lax.broadcasted_iota(jnp.int32, (8, PB), 0)
        row = lax.broadcasted_iota(jnp.int32, (PB, PB), 0)
        lane = lax.broadcasted_iota(jnp.int32, (PB, PB), 1)
        work[:, :PB] = a_ref[...]
        work[:, PB:] = (row == lane).astype(F32)

        def spread_row(value, s):
            return jnp.broadcast_to(value[s : s + 1, :], (8, PB))

        @pl.loop(0, PB // 8)
        def _(step):
            at = pl.ds(pl.multiple_of(step * 8, 8), 8)
            left, right = work[at, :PB], work[at, PB:]
            near = pltpu.roll(left, (PB - step * 8) % PB, 1)
            columns = [jnp.broadcast_to(near[:, c : c + 1], (8, PB)) for c in range(8)]
            for s in range(8):
                scale = lax.rsqrt(spread_row(columns[s], s))
                row_left = spread_row(left, s) * scale
                row_right = spread_row(right, s) * scale
                weight = jnp.where(sub > s, columns[s] * scale, 0.0)
                left = jnp.where(sub == s, row_left, left - weight * row_left)
                right = jnp.where(sub == s, row_right, right - weight * row_right)
                for c in range(s + 1, 8):
                    columns[c] = columns[c] - weight * (spread_row(columns[s], c) * scale)
            o_ref[at, :] = right
            both = jnp.concatenate([left, right], 1)
            work[...] -= lax.dot_general(
                left, both, CELLS_FIRST, precision=HIGHEST, preferred_element_type=F32
            )

    return pl.pallas_call(
        body,
        out_shape=jax.ShapeDtypeStruct((PB, PB), F32),
        scratch_shapes=[pltpu.VMEM((PB, 2 * PB), F32)],
        cost_estimate=pl.CostEstimate(
            flops=8 << 30, bytes_accessed=PB * PB * 8, transcendentals=PB
        ),
        name="inverse_factor",
    )(block)


def finish(zfield, chunks, solves, factor, info, pair, slot_of):
    cells, width = zfield.shape
    lines = cells // NY
    block = 2 * PB if pair else PB
    arrays = []
    for array, _ in chunks:
        if not any(array is known for known in arrays):
            arrays.append(array)
    index = lambda array: [array is known for known in arrays].index(True)

    def body(t, *refs):
        hbm, rest = refs[: len(arrays)], refs[len(arrays) :]
        z_ref, one_ref, cross_ref, two_ref, f_ref, out_ref, half_ref = rest[:7]
        got_ref, pan_ref, bas_ref, sems = rest[7:]
        step = pl.program_id(0)
        role = t[0]

        def copy_of(slot):
            array, column = chunks[slot]
            return pltpu.make_async_copy(
                hbm[index(array)].at[:, column : column + block], got_ref.at[slot], sems.at[slot]
            )

        @pl.when(step == 0)
        def _():
            for slot in range(lines):
                copy_of(slot).start()

        mine = slot_of(step, t)
        for slot in range(lines):

            @pl.when(mine == slot)
            def _():
                copy_of(slot).wait()

        def tile(which):
            return z_ref[:, pl.ds(pl.multiple_of(t[which] * PB, PB), PB)]

        @pl.when(role == 0)
        def _():
            pan_ref[:, :PB] = tile(1)
            pan_ref[:, PB:] = tile(2) if pair else got_ref[mine]

        @pl.when(role != 0)
        def _():
            if pair:
                pan_ref[...] = got_ref[mine]
            else:
                pan_ref[:, :PB] = got_ref[mine]
                pan_ref[:, PB:] = tile(1)

        one = lax.dot_general(
            pan_ref[:, :PB], one_ref[...], LAST_LAST, preferred_element_type=F32
        ).astype(BF16)
        partial = (
            pan_ref[:, PB:].astype(F32)
            - lax.dot_general(one, cross_ref[...], LAST_LAST, preferred_element_type=F32)
        ).astype(BF16)
        two = lax.dot_general(
            partial, two_ref[...], LAST_LAST, preferred_element_type=F32
        ).astype(BF16)
        bas_ref[:, :PB] = one
        bas_ref[:, PB:] = two
        out_ref[...] = (
            z_ref[...].astype(F32)
            - lax.dot_general(
                bas_ref[...], f_ref[...], LAST_LAST, preferred_element_type=F32
            )
        ).astype(BF16)

        @pl.when(step // (lines // 2) == t[3])
        def _():
            half_ref[...] = bas_ref[...]

    small = pl.BlockSpec((PB, PB), lambda j, t: (0, 0))
    line = pl.BlockSpec((NY, width), lambda j, t: (j, 0))
    last = lines // 2 - 1
    return pl.pallas_call(
        body,
        grid_spec=pltpu.PrefetchScalarGridSpec(
            num_scalar_prefetch=1,
            grid=(lines,),
            in_specs=[pl.BlockSpec(memory_space=pl.ANY)] * len(arrays)
            + [line, small, small, small, pl.BlockSpec((width, 2 * PB), lambda j, t: (0, 0))],
            out_specs=[
                line,
                pl.BlockSpec(
                    (NY, 2 * PB), lambda j, t: (jnp.clip(j - t[3] * (last + 1), 0, last), 0)
                ),
            ],
            scratch_shapes=[
                pltpu.VMEM((lines, NY, block), BF16),
                pltpu.VMEM((NY, 2 * PB), BF16),
                pltpu.VMEM((NY, 2 * PB), BF16),
                pltpu.SemaphoreType.DMA((lines,)),
            ],
        ),
        out_shape=[
            jax.ShapeDtypeStruct((cells, width), BF16),
            jax.ShapeDtypeStruct((cells // 2, 2 * PB), BF16),
        ],
        compiler_params=pltpu.CompilerParams(vmem_limit_bytes=VMEM_BYTES),
        cost_estimate=LITTLE,
        name="finish",
    )(info, *arrays, zfield, *solves, factor)


def swap(value):
    return lax.ppermute(value, "cols", SWAP)


def bit_of(bit):
    return lax.axis_index("rows") // bit % 2


def row_bits():
    count = lax.axis_size("rows")
    return [1 << k for k in range(count.bit_length() - 1)]


def over_rows(value, bit):
    count = lax.axis_size("rows")
    return lax.ppermute(value, "rows", [(k, k ^ bit) for k in range(count)])


def sum_rows(value):
    for bit in row_bits():
        value = value + over_rows(value, bit)
    return value


def reduce_rows(split, whole=None):
    for bit in row_bits():
        half = split.shape[0] // 2
        side = bit_of(bit)
        keep = lax.dynamic_slice_in_dim(split, side * half, half, 0)
        send = lax.dynamic_slice_in_dim(split, (1 - side) * half, half, 0)
        if whole is None:
            split = keep + over_rows(send, bit)
        else:
            got = over_rows(jnp.concatenate([send, whole], 0), bit)
            split = keep + got[:half]
            whole = whole + got[half:]
    return split, whole


def slice_start(width):
    start = 0
    for bit in row_bits():
        width //= 2
        start = start + bit_of(bit) * width
    return start


def gather_rows(value):
    for bit in reversed(row_bits()):
        other = over_rows(value, bit)
        value = jnp.where(
            bit_of(bit) == 0,
            jnp.concatenate([value, other], 0),
            jnp.concatenate([other, value], 0),
        )
    return value


def dot_t(left, right):
    return lax.dot_general(left, right, LAST_LAST, precision=HIGHEST, preferred_element_type=F32)


def step_of(live, work, *values):
    shapes = jax.eval_shape(work, *values)
    empty = lambda *_: jax.tree.map(lambda shape: jnp.zeros(shape.shape, shape.dtype), shapes)
    return lax.cond(live, work, empty, *values)


def after(value, *events):
    return lax.optimization_barrier((value, *events))[0]


def two_groups(sketch, stiffness, reaction, panel_order):
    cells, width = sketch.shape
    lines = cells // NY
    panels_here = width // PB
    row_count = lax.axis_size("rows")
    scale = 1.0 / (cells * row_count)
    group = lax.axis_index("cols")
    first, second = panel_order[0], panel_order[1]
    group_one, group_two = first // panels_here, second // panels_here
    share = width // row_count
    eye = jnp.eye(PB, dtype=F32)
    tile_one = first % panels_here
    tile_two = second % panels_here
    holds_one = group == group_one
    role = jnp.where(holds_one, 0, 1)

    def upward(value):
        return lax.ppermute(value, "rows", [(i, i + 1) for i in range(row_count - 1)])

    def downward(value):
        return lax.ppermute(value, "rows", [(i + 1, i) for i in range(row_count - 1)])

    def identity_rows(panel):
        position = group * width + slice_start(width) + jnp.arange(share, dtype=jnp.int32)
        offset = jnp.arange(PB, dtype=jnp.int32)
        return (position[:, None] == panel * PB + offset[None, :]).astype(F32)

    def factor_of(one, two, inverse_one, cross, inverse_two):
        core_one = one * scale + identity_rows(first)
        core_two = two * scale + identity_rows(second)
        column_one = dot_t(core_one, inverse_one)
        column_two = dot_t(core_two - dot_t(column_one, cross), inverse_two)
        return gather_rows(jnp.concatenate([column_one, column_two], 1))

    def apart(sketch, mix, stiff, info):
        def order(slot, turned):
            turned = jnp.asarray(turned, jnp.int32)
            near = (slot + 1) & 3
            return jnp.where((slot < 4) == (turned == 0), near, (slot & 3) + 4)

        def sent(slot):
            return lambda j, t: order(slot + j, t[0])

        def came(slot):
            return lambda j, t: order(slot + j, 1 - t[0])

        own_tile = lambda j, t: t[1]
        tile_after = lambda j, t: (t[1] + 1 + j) % panels_here
        bottom, top = lambda j, t: lines - 1, lambda j, t: 0
        inner = lambda j: jnp.where(j < 3, j, j + 1)
        early = panel_lines(
            sketch, mix, stiff, info, 6, lambda j, t: order(inner(j), t[0]), own_tile
        )
        got_early = swap(early)
        others = panels_here - 1

        live = info[3] >= 0
        def halo_copies(own, rest):
            copies = [(own, 0, 0, PB, lambda t: t[1] * PB)]
            for j in range(others):
                copies.append((rest, 0, j * PB, PB, lambda t, j=j: tile_after(j, t) * PB))
            return copies

        def local_field(sketch, mix, stiff, info):
            low_own, high_own, low_rest, high_rest = take_halos(
                sketch, info, own_tile, tile_after
            )
            low_own, high_own = upward(low_own), downward(high_own)
            low_rest, high_rest = upward(low_rest), downward(high_rest)
            edges = panel_lines(
                sketch,
                mix,
                stiff,
                info,
                2,
                lambda j, t: order(3 + 4 * j, t[0]),
                own_tile,
                low_own,
                high_own,
            )
            low, high = halo_copies(low_own, low_rest), halo_copies(high_own, high_rest)
            return edges, *whole_field(sketch, mix, stiff, info, 1, low, high)

        edges, zfield, own = step_of(
            live, local_field, after(sketch, early), mix, stiff, info
        )
        got_edges = swap(edges)
        many = gram_parts(
            zfield,
            [(got_early, 6)],
            info,
            lambda j, t: order(inner(j), 1 - t[0]),
        )
        few = gram_parts(
            zfield,
            [(after(got_edges, many), 2)],
            info,
            lambda j, t: order(3 + 4 * j, 1 - t[0]),
        )

        def all_sums(own, other, info):
            own_rows = lambda value: lax.dynamic_slice_in_dim(value, info[1] * PB, PB, 0)
            both = jnp.concatenate([own, other], 1)
            shares, whole = reduce_rows(both, own_rows(both))
            own_share, other_share = shares[:, :PB], shares[:, PB:]
            diag_own, mixed_own = whole[:, :PB], whole[:, PB:]
            inverse_own = inverse_factor(diag_own * scale + eye)
            got = swap(jnp.where(holds_one, inverse_own, diag_own))
            inverse_one = jnp.where(holds_one, inverse_own, got)
            diag_two = jnp.where(holds_one, got, diag_own)
            cross = dot_t(jnp.where(holds_one, mixed_own.T, mixed_own) * scale, inverse_one)
            inverse_two = inverse_factor(diag_two * scale + eye - dot_t(cross, cross))
            one = jnp.where(holds_one, own_share, other_share)
            two = jnp.where(holds_one, other_share, own_share)
            factor = factor_of(one, two, inverse_one, cross, inverse_two)
            return factor, inverse_one, cross, inverse_two

        factor, inverse_one, cross, inverse_two = step_of(live, all_sums, own, many + few, info)

        def slot_of(line, t):
            near = (line + 3) & 3
            return jnp.where(
                t[0] == 0, jnp.where(line < 4, near + 4, line - 4), jnp.where(line < 4, near, line)
            )

        solves = [value.astype(BF16) for value in (inverse_one, cross, inverse_two)]
        chunks = [(got_early, 0), (got_early, PB), (got_early, 2 * PB), (got_edges, 0)]
        chunks += [(got_early, 3 * PB), (got_early, 4 * PB), (got_early, 5 * PB), (got_edges, PB)]
        residual, basis_rows = finish(
            zfield, chunks, solves, factor.astype(BF16), info, False, slot_of
        )
        return residual, basis_rows, factor

    def together(sketch, mix, stiff, info):
        owner = holds_one
        pairs = [(1, 2), (3, 4), (0, 7), (5, 6)]

        def tile_at(j, t):
            return jnp.where(j % 2 == 0, t[1], t[2])

        def chunk(near, far):
            return panel_lines(
                sketch,
                mix,
                stiff,
                info,
                4,
                lambda j, t: jnp.where(t[0] == 0, near + j // 2, far),
                lambda j, t: jnp.where(t[0] == 0, tile_at(j, t), j),
            )

        chunk_one = chunk(1, 5)
        got_one = swap(chunk_one)
        chunk_two = chunk(3, 6)
        got_two = swap(chunk_two)
        live = info[3] >= 0
        nothing = lambda j, t: 0
        whole_line = lambda halo: [(halo, 0, 0, width, lambda t: 0)]

        def local_field(sketch, mix, stiff, info):
            low = upward(copy_lines(sketch, info, 1, lambda j, t: lines - 1, nothing, width))
            high = downward(copy_lines(sketch, info, 1, nothing, nothing, width))
            zfield, own = whole_field(
                sketch, mix, stiff, info, 2, whole_line(low), whole_line(high)
            )
            return zfield, own, copy_lines(zfield, info, 4, lambda j, t: j // 2 * 7, tile_at)

        sketch = after(sketch, chunk_one, chunk_two)
        zfield, own, chunk_three = step_of(live, local_field, sketch, mix, stiff, info)
        got_three = swap(chunk_three)

        def owner_part(zfield, received, line, info):
            return gram_lines(
                received,
                [
                    (zfield, PB, lambda j, t: (line, t[1])),
                    (zfield, PB, lambda j, t: (line, t[2])),
                ],
                info,
                1,
                lambda j, t: 0,
            )

        def other_part(zfield, received, pair, info):
            return gram_lines(
                zfield,
                [(received, 2 * PB, lambda j, t: (0, j))],
                info,
                2,
                lambda j, t: pair[0] + j * (pair[1] - pair[0]),
            )

        def own_sums(own, owner_sum, info):
            shares, _ = reduce_rows(jnp.concatenate([own, owner_sum], 1))
            own_share, owner_share = shares[:, : 2 * PB], shares[:, 2 * PB :]
            total = gather_rows(own_share)
            return own_share, owner_share, *[
                lax.dynamic_slice_in_dim(total, info[k] * PB, PB, 0) for k in (1, 2)
            ]

        own = after(own, chunk_three)
        owner_sum = owner_part(zfield, got_one, 5, info)
        other_sum = other_part(zfield, got_one, pairs[0], info)
        late_two = after(got_two, owner_sum, other_sum)
        owner_sum = owner_sum + owner_part(zfield, late_two, 6, info)
        own_share, owner_share, diag_one, diag_two = step_of(live, own_sums, own, owner_sum, info)
        small = jnp.concatenate([diag_one, diag_two, owner_share], 0)
        got_small = swap(small)
        chunk_four = copy_lines(zfield, info, 4, lambda j, t: 5 + j // 2, tile_at)
        got_four = swap(after(chunk_four, got_small))
        other_sum = other_sum + other_part(zfield, after(late_two, small), pairs[1], info)
        other_sum = other_sum + other_part(zfield, after(got_three, small), pairs[2], info)
        diag = jnp.where(owner, small[: 2 * PB], got_small[: 2 * PB])
        extra = got_small[2 * PB :]

        def last_sums(other_sum, own_share, extra, diag):
            inverse_one = inverse_factor(diag[:PB, :PB] * scale + eye)
            cross = dot_t(diag[PB:, :PB] * scale, inverse_one)
            inverse_two = inverse_factor(diag[PB:, PB:] * scale + eye - dot_t(cross, cross))
            other_share, _ = reduce_rows(other_sum)
            mine = jnp.where(owner, own_share, other_share + extra)
            factor = factor_of(mine[:, :PB], mine[:, PB:], inverse_one, cross, inverse_two)
            return factor, inverse_one, cross, inverse_two

        factor, inverse_one, cross, inverse_two = step_of(
            live, last_sums, after(other_sum, chunk_four), own_share, extra, diag
        )

        def slot_of(line, t):
            return jnp.where(line == 0, 4, jnp.where(line == 7, 5, jnp.where(line < 5, line - 1, line + 1)))

        solves = [value.astype(BF16) for value in (inverse_one, cross, inverse_two)]
        chunks = [
            (array, column)
            for array in (got_one, got_two, got_three, after(got_four, factor))
            for column in (0, 2 * PB)
        ]
        residual, basis_rows = finish(
            zfield, chunks, solves, factor.astype(BF16), info, True, slot_of
        )
        return residual, basis_rows, factor

    stiff = stiffness.reshape(-1, LANES)
    mix = (reaction + 4.0 * stiffness).reshape(-1, LANES)
    same = group_one == group_two
    info = jnp.stack(
        [
            role,
            jnp.where(same | holds_one, tile_one, tile_two),
            jnp.where(same | (role == 1), tile_two, tile_one),
            group,
        ]
    ).astype(jnp.int32)
    return lax.cond(same, together, apart, sketch, mix, stiff, info)


def per_device(sketch, stiffness, reaction, panel_order):
    cells, width = sketch.shape
    rows = lax.axis_size("rows")
    fits = lax.axis_size("cols") == 2 and cells == 8 * NY and width == 4 * PB
    if fits and rows & (rows - 1) == 0 and rows > 1:
        return two_groups(sketch, stiffness, reaction, panel_order)
    return any_groups(sketch, stiffness, reaction, panel_order)


def solution(mesh):
    return jax.shard_map(
        per_device,
        mesh=mesh,
        in_specs=(P("rows", "cols"), P("rows"), P("rows"), P()),
        out_specs=(P("rows", "cols"), P(("rows", "cols"), None), P("cols", None)),
        check_vma=False,
    )
```
